256 devices in a mesh: env: 16 (over x, y_lo, core), pts: 16 (over y_hi, z).
Axes of the slice: x: 4, y: 4 (y_hi: 2, y_lo: 2; y = y_hi * 2 + y_lo), z: 8, core: 2. Of those that a mesh axis runs over, the one named last changes fastest.
Arguments:
- descriptors: float32 [1024, 16384], P('pts', 'env'), may hold values from -6 to 6
- env_weight: float32 [16384], P('env'), may hold values from 0.25 to 4
- points: float32 [2560, 1024], P('pts', 'env'), may hold values from -6 to 6
Outputs:
- panel_factor: float32 [2560, 512], P('env', 'pts')
- trailing: float32 [2048, 2048], P('env', 'pts')
The draws below stay inside these ranges and needn't reach their ends.
All inputs are finite; a program needn't handle non-finite values.
Results may differ from the reference program's by a relative error of at most 0.0003.
Values sent between devices are 32-bit elements; how exact they have to be, the bound alone decides.
A program may use at most 64 MiB of HBM per device.

```python
import math
import jax
import jax.numpy as jnp
from jax import lax

D = 1024
PANEL = 512
TRAIL = 2048
NENV = 16384
NPTS = 2560
N_ENV = 16
N_PTS = 16


def block_scale(key, shape, shards, low, high):
    gain, own = 1.0, jax.random.fold_in(key, 6)
    for axis_at, parts in shards:
        draws = jnp.exp(jax.random.uniform(jax.random.fold_in(own, axis_at), (parts,), jnp.float32, low / len(shards), high / len(shards)))
        gain = gain * jnp.repeat(draws, shape[axis_at] // parts).reshape([-1 if axis == axis_at else 1 for axis in range(len(shape))])
    return gain


def centred(rng, dims, spread, bound, split=(), held_as=jnp.bfloat16):
    level = block_scale(rng, dims, split, -0.22, 0.18) if split else 1.0
    array = jax.random.normal(rng, dims, jnp.float32) * spread * level
    return jnp.minimum(jnp.maximum(array, -bound), bound).astype(held_as)


def setup_inputs(seed: int = 0) -> dict:
    seeds = jax.random.split(jax.random.key(seed), 4)
    return {
        "descriptors": centred(seeds[0], (D, NENV), 1.0, 6.0, ((0, 16), (1, 16)), jnp.float32),
        "env_weight": jnp.clip(jnp.exp(math.log(4.0) - 2.7725887 * jax.random.uniform(seeds[1], (NENV,), jnp.float32) ** block_scale(seeds[1], (NENV,), ((0, 16),), -0.2, 0.2)), 0.25, 4.0),
        "points": centred(seeds[2], (NPTS, D), 1.0, 6.0, ((0, 16), (1, 16)), jnp.float32),
    }


def cubed_kernel(features, targets):
    dots = lax.dot_general(features.astype(jnp.float32), targets.astype(jnp.float32), (((0,), (1,)), ((), ())), precision=lax.Precision.HIGHEST, preferred_element_type=jnp.float32)
    scaled = dots / jnp.sqrt(jnp.float32(features.shape[0]))
    return 0.25 * scaled * scaled * scaled

def natural_index(count, devices, skipped):
    per_device = count // devices
    block_size = PANEL // devices
    positions = jnp.arange(count, dtype=jnp.int32)
    device = positions // per_device
    local = positions % per_device + skipped * block_size
    return (block_size * (devices * (local // block_size) + device) + local % block_size).astype(jnp.int32)

def reference(descriptors, env_weight, points):
    column_ids = natural_index(NPTS, N_PTS, 0)
    ordered = jnp.zeros_like(points).at[column_ids].set(points)
    kernel = cubed_kernel(descriptors, ordered)
    weighted = kernel * env_weight[:, None]
    gram = lax.dot_general(weighted.astype(jnp.float32), kernel.astype(jnp.float32), (((0,), (0,)), ((), ())), precision=lax.Precision.HIGHEST, preferred_element_type=jnp.float32)
    gram = gram / NENV + jnp.eye(NPTS, dtype=jnp.float32)
    low_factor = jnp.linalg.cholesky(gram[:PANEL, :PANEL])
    factor = jax.scipy.linalg.solve_triangular(low_factor, gram[:, :PANEL].T, lower=True).T
    row_ids = natural_index(NPTS, N_ENV, 0)
    panel_factor = factor[row_ids]
    tail_factor = factor[PANEL:]
    schur = gram[PANEL:, PANEL:] - jnp.dot(tail_factor.astype(jnp.float32), tail_factor.T.astype(jnp.float32), precision=lax.Precision.HIGHEST, preferred_element_type=jnp.float32)
    trail_rows = natural_index(TRAIL, N_ENV, 1) - PANEL
    trail_cols = natural_index(TRAIL, N_PTS, 1) - PANEL
    trailing = schur[trail_rows][:, trail_cols]
    return (panel_factor, trailing)
```

```python
import jax
import jax.numpy as jnp
from jax import lax
from jax.sharding import Mesh
from jax.sharding import PartitionSpec as P

PANEL = 512
PTS = ("pts_0", "pts_1")
ENV_PTS = ("env", "pts_0", "pts_1")


def joined_along(blocks, dim):
    lengths = list(blocks.shape[1:])
    lengths[dim] *= blocks.shape[0]
    return jnp.moveaxis(blocks, 0, dim).reshape(lengths)


def gather_in_order(shard, axes, order):
    blocks = shard[None]
    for k in order:
        blocks = lax.all_gather(blocks, axes[k], axis=0, tiled=True)
    held = [lax.axis_size(axes[k]) for k in reversed(order)]
    blocks = blocks.reshape(*held, *shard.shape)
    turned = sorted(range(len(order)), key=lambda place: order[len(order) - 1 - place])
    return blocks.transpose(*turned, *range(len(order), blocks.ndim)).reshape(-1, *shard.shape)


def gathered_by_axis(shard, axes, order, dim):
    return joined_along(gather_in_order(shard, axes, order), dim)


def cut_along(shard, dim, count):
    before, after = (shard.shape[:dim], shard.shape[dim + 1 :])
    return jnp.moveaxis(shard.reshape(*before, count, -1, *after), dim, 0)


def summed_on_arrival(shard, axis, dim):
    count = lax.axis_size(axis)
    blocks = lax.all_to_all(cut_along(shard, dim, count), axis, 0, 0, tiled=True)
    return jnp.sum(blocks, axis=0)


def cubed_kernel(features, targets):
    dots = lax.dot_general(
        features,
        targets,
        (((0,), (1,)), ((), ())),
        precision=lax.Precision.HIGH,
        preferred_element_type=jnp.float32,
    )
    scaled = dots / jnp.sqrt(jnp.float32(features.shape[0]))
    return 0.25 * scaled * scaled * scaled


def local_points(count, device, devices, block_size):
    positions = jnp.arange(count, dtype=jnp.int32)
    return block_size * (devices * (positions // block_size) + device) + positions % block_size


def local(descriptors, env_weight, points):
    env_count = lax.axis_size("env")
    pts_count = lax.axis_size(PTS)
    env_rank = lax.axis_index("env")
    pts_rank = lax.axis_index(PTS)
    features = gathered_by_axis(descriptors, PTS, (0, 1), 0)
    own_points = lax.all_gather(points, "env", axis=1, tiled=True)
    cols_dev = own_points.shape[0]
    total_points = cols_dev * pts_count
    rows_dev = total_points // env_count
    row_block = PANEL // env_count
    col_block = PANEL // pts_count
    cycles = total_points // PANEL
    own_tile = cubed_kernel(features, own_points)
    weighted = own_tile * env_weight[:, None]
    partial_gram = lax.dot_general(
        lax.all_gather(own_tile, PTS, axis=1, tiled=True),
        weighted,
        (((0,), (0,)), ((), ())),
        precision=lax.Precision.HIGH,
        preferred_element_type=jnp.float32,
    )
    partial_gram = partial_gram / jnp.float32(descriptors.shape[1] * env_count)
    natural = (
        partial_gram.reshape(pts_count, cycles, col_block, cols_dev)
        .transpose(1, 0, 2, 3)
        .reshape(total_points, cols_dev)
    )
    by_rows = (
        natural.reshape(cycles, env_count, row_block, cols_dev)
        .transpose(1, 0, 2, 3)
        .reshape(total_points, cols_dev)
    )
    gram_block = summed_on_arrival(by_rows, "env", 0)
    row_ids = local_points(rows_dev, env_rank, env_count, row_block)
    col_ids = local_points(cols_dev, pts_rank, pts_count, col_block)
    gram_block = gram_block + (row_ids[:, None] == col_ids[None, :]).astype(jnp.float32)
    panel_rows = lax.all_gather(gram_block[:, :col_block], PTS, axis=1, tiled=True)
    leading = lax.all_gather(panel_rows[:row_block], "env", axis=0, tiled=True)
    low_factor = jnp.linalg.cholesky(leading)
    row_factor = jax.scipy.linalg.solve_triangular(low_factor, panel_rows.T, lower=True).T
    panel_out = lax.dynamic_slice_in_dim(row_factor, pts_rank * col_block, col_block, 1)
    top_rows = lax.all_gather(gram_block[:row_block, :], "env", axis=0, tiled=True)
    side_factor = jax.scipy.linalg.solve_triangular(low_factor, top_rows, lower=True).T[col_block:]
    update = lax.dot_general(
        row_factor[row_block:],
        side_factor,
        (((1,), (1,)), ((), ())),
        precision=lax.Precision.HIGHEST,
        preferred_element_type=jnp.float32,
    )
    trailing = gram_block[row_block:, col_block:] - update
    return (panel_out, trailing)


def solution(mesh):
    finer = Mesh(mesh.devices.reshape(mesh.shape["env"], 2, 8), ("env", "pts_0", "pts_1"))
    placed = (P(PTS, "env"), P("env"), P(PTS, "env"))
    return jax.shard_map(
        local,
        mesh=finer,
        in_specs=placed,
        out_specs=(P("env", PTS), P("env", PTS)),
        check_vma=False,
    )
```

```python
import functools

import jax
import jax.numpy as jnp
from jax import lax
from jax.experimental import pallas as pl
from jax.experimental.pallas import tpu as pltpu
from jax.sharding import PartitionSpec as P

MESH = pl.DeviceIdType.MESH
HI = lax.Precision.HIGHEST
F32 = jnp.float32
BF16 = jnp.bfloat16
NB = 128
NENV = 16384
OFFSETS = (0, 1, 2, 4)


def placed():
    e, p = lax.axis_index("env"), lax.axis_index("pts")
    x, y_lo, c = e // 4, (e // 2) % 2, e % 2
    y_hi, z = p // 8, p % 8
    return e, p, x, 2 * y_hi + y_lo, z, c


def device(x, y, z, c):
    return (4 * x + 2 * (y % 2) + c, 8 * (y // 2) + z)


def remote(src, dst, send_sem, recv_sem, to):
    return pltpu.make_async_remote_copy(
        src_ref=src, dst_ref=dst, send_sem=send_sem, recv_sem=recv_sem, device_id=to, device_id_type=MESH
    )


def arrived(ref, sem):
    pltpu.make_async_copy(ref, ref, sem).wait()


def halves(a):
    hi = a.astype(BF16)
    return hi, (a - hi.astype(F32)).astype(BF16)


def dot3(a, b, dims):
    one = lambda l, r: lax.dot_general(l, r, (dims, ((), ())), preferred_element_type=F32)
    return one(a[0], b[0]) + (one(a[0], b[1]) + one(a[1], b[0]))


def gather_and_multiply(
    desc, points, weight, tt_out, panel_out,
    half, other_weight, line, table, feats, feats_hi, feats_lo, rows_hi, rows_lo, kp, kt,
    half_s, half_r, swap_s, swap_r, local_s, zp_s, zp_r, zt_s, zt_r, slab_s, slab_r, slabx_s, slabx_r,
    ring_s, ring_r, ringx_s, ringx_r,
):
    e, p, x, y, z, c = placed()
    h = p // 8
    native = c == h
    turn = jnp.where(native, 1, 7)
    sibling = device(x, y, z, 1 - c)
    partner = device(x, (y + 2) % 4, z, 1 - c)
    along_z = lambda d: device(x, y, (z + d) % 8, c)

    def step(j1, j2):
        return (x + j1 * (1 - c) + j2 * c) % 4, (y + j1 * c + j2 * (1 - c)) % 4

    def slab_of(j1, j2, core):
        sx = (x + 8 - j1 * (1 - core) - j2 * core) % 4
        sy = (y + 8 - j1 * core - j2 * (1 - core)) % 4
        lanes = pl.multiple_of(128 * (2 * sx + sy % 2), 128)
        return table.at[sy // 2, core, :, pl.ds(lanes, 128)]

    barrier = pltpu.get_barrier_semaphore()
    greet = [sibling, partner] + [along_z(d) for d in range(1, 8)]
    greet += [device(*step(j, 0), z, c) for j in (1, 2, 3)] + [device(*step(0, j), z, c) for j in (1, 2, 3)]
    for who in greet:
        pl.semaphore_signal(barrier, inc=1, device_id=who, device_id_type=MESH)
    pl.semaphore_wait(barrier, len(greet))

    o = 1 - c
    to_sibling = [
        remote(points.at[pl.ds(pl.multiple_of(16 * o, 16), 16)], half.at[0:16], half_s.at[0], half_r.at[0], sibling),
        remote(points.at[pl.ds(pl.multiple_of(32 + 64 * o, 32), 64)], half.at[16:80], half_s.at[1], half_r.at[1], sibling),
        remote(weight, other_weight, half_s.at[2], half_r.at[2], sibling),
    ]
    for copy in to_sibling:
        copy.start()
    swap = remote(desc, feats.at[p], swap_s, swap_r, partner)
    keep = pltpu.make_async_copy(desc, feats.at[p], swap_r)

    @pl.when(native)
    def _():
        keep.start()

    @pl.when(jnp.logical_not(native))
    def _():
        swap.start()

    arrived(half.at[0:16], half_r.at[0])
    arrived(half.at[16:80], half_r.at[1])
    mine = jnp.concatenate(
        [points[pl.ds(pl.multiple_of(16 * c, 16), 16)], points[pl.ds(pl.multiple_of(32 + 64 * c, 32), 64)]], axis=0
    )
    theirs = half[...]
    packed = jnp.where(c == 0, jnp.concatenate([mine, theirs], axis=1), jnp.concatenate([theirs, mine], axis=1))
    own_panel = line.at[pl.ds(pl.multiple_of(16 * z, 16), 16)]
    line[pl.ds(pl.multiple_of(16 * z, 16), 16)] = packed[0:16]
    line[128:192] = packed[16:80]

    lined = []
    for s in (1, 2, 3):
        rows = pl.ds(128 + 64 * s, 64)
        lined.append(remote(line.at[128:192], line.at[rows], zt_s.at[s], zt_r.at[s], along_z(8 - OFFSETS[s])))
    for d in range(1, 8):
        lined.append(remote(own_panel, own_panel, zp_s.at[d], zp_r.at[d], along_z(d)))
    for copy in lined:
        copy.start()

    def piece(m, core, sign):
        d = (0, 1, 2, 3, 4, 7, 6, 5)[m]
        return feats.at[8 * core + (z + 8 * 8 - sign * d) % 8]

    rings, across = [], []

    def pass_on(m):
        src = piece(m, c, turn)
        if m in (0, 1, 2, 3):
            copy = remote(src, src, ring_s.at[m + 1], ring_r.at[m + 1], along_z(turn))
            copy.start()
            rings.append(copy)
        if m in (0, 5, 6):
            n = 5 if m == 0 else m + 1
            copy = remote(src, src, ring_s.at[n], ring_r.at[n], along_z(8 - turn))
            copy.start()
            rings.append(copy)
        copy = remote(src, src, ringx_s.at[m], ringx_r.at[m], sibling)
        copy.start()
        across.append(copy)

    arrived(piece(0, c, turn), swap_r)
    pass_on(0)

    for s in (1, 2, 3):
        arrived(line.at[pl.ds(128 + 64 * s, 64)], zt_r.at[s])
    for d in range(1, 8):
        rows = pl.ds(pl.multiple_of(16 * ((z + 8 - d) % 8), 16), 16)
        arrived(line.at[rows], zp_r.at[d])

    slabs = []

    def spread(j1, src, dst):
        if j1 == 0:
            for j in (1, 2, 3):
                slabs.append(remote(src, dst, slab_s.at[4 * j], slab_r.at[4 * j], device(*step(j, 0), z, c)))
                slabs[-1].start()
        for j in (1, 2, 3):
            n = 4 * j1 + j
            slabs.append(remote(src, dst, slab_s.at[n], slab_r.at[n], device(*step(0, j), z, c)))
            slabs[-1].start()

    def to_other_core(n, src, dst):
        slabs.append(remote(src, dst, slabx_s.at[n], slabx_r.at[n], sibling))
        slabs[-1].start()

    own = slab_of(0, 0, c)
    spread(0, line, own)
    to_other_core(0, line, own)
    stay = pltpu.make_async_copy(line, own, local_s)
    stay.start()

    def take_piece(m):
        arrived(piece(m, c, turn), ring_r.at[m])
        pass_on(m)

    def take_slab(j1, j2):
        here = slab_of(j1, j2, c)
        arrived(here, slab_r.at[4 * j1 + j2])
        if j2 == 0:
            spread(j1, here, here)
        to_other_core(4 * j1 + j2, here, here)

    take_slab(1, 0)
    take_slab(3, 0)
    take_piece(1)
    take_piece(5)
    take_slab(2, 0)
    take_slab(0, 1)
    take_slab(0, 3)
    take_slab(0, 2)
    take_piece(2)
    take_piece(6)
    for j1 in (1, 3):
        for j2 in (1, 3, 2):
            take_slab(j1, j2)
    take_piece(3)
    take_piece(7)
    for j2 in (1, 3, 2):
        take_slab(2, j2)
    take_piece(4)

    for m in range(8):
        arrived(piece(m, o, 8 - turn), ringx_r.at[m])
    for j1 in range(4):
        for j2 in range(4):
            arrived(slab_of(j1, j2, o), slabx_r.at[4 * j1 + j2])
    stay.wait()
    arrived(other_weight, half_r.at[2])
    for copy in to_sibling + lined + rings + across + slabs:
        copy.wait_send()

    @pl.when(jnp.logical_not(native))
    def _():
        swap.wait_send()

    def split_feats(i, carry):
        hi, lo = halves(feats[i])
        rows = pl.ds(pl.multiple_of(64 * i, 64), 64)
        feats_hi[rows] = hi
        feats_lo[rows] = lo
        return carry

    lax.fori_loop(0, 16, split_feats, 0)

    def kernel_rows(i, carry):
        hh, cc = i // 2, i % 2
        hi, lo = halves(table[hh, cc, 0:256])
        rows_hi[0:256], rows_lo[0:256] = hi, lo
        hi, lo = halves(table[hh, cc, pl.ds(pl.multiple_of(256 + 64 * c, 64), 64)])
        rows_hi[256:320], rows_lo[256:320] = hi, lo

        def columns(t, carry):
            lanes = pl.ds(pl.multiple_of(256 * t, 256), 256)
            scaled = dot3(
                (rows_hi[...], rows_lo[...]), (feats_hi[:, lanes], feats_lo[:, lanes]), ((1,), (0,))
            ) * (1.0 / 32.0)
            value = 0.25 * scaled * scaled * scaled
            for zz in range(8):
                at = pl.multiple_of(256 * hh + 32 * zz + 16 * cc, 16)
                kp[pl.ds(at, 16), lanes] = value[16 * zz : 16 * zz + 16]
            for s in range(3):
                at = pl.multiple_of(128 * hh + 64 * cc, 64)
                kt[s, pl.ds(at, 64), lanes] = value[128 + 64 * s : 192 + 64 * s]
            return carry

        lax.fori_loop(0, 4, columns, 0)
        return carry

    lax.fori_loop(0, 4, kernel_rows, 0)

    w = jnp.where(native, weight[0:1], other_weight[0:1]) * (1.0 / NENV)
    nt = ((1,), (1,))

    def unit(k, carry):
        first = (k + 1) // 2
        row = jnp.where(first == 1, c, 0)
        col = jnp.where(first == 0, 0, jnp.where(first == 1, 1 + c, 2))
        side = jnp.where(first == 0, c, (k + 1) % 2)
        a = halves(kt[row] * w)
        b = halves(kt[col, pl.ds(pl.multiple_of(128 * side, 128), 128)])
        tt_out[k] = dot3(a, b, nt)
        return carry

    lax.fori_loop(0, 5, unit, 0)
    trail = halves(kt[0, pl.ds(pl.multiple_of(128 * c, 128), 128)] * w)
    lead = halves(kp[pl.ds(pl.multiple_of(256 * c + 32 * z, 32), 32)] * w)

    def panel(i, carry):
        a = halves(kp[pl.ds(pl.multiple_of(128 * i, 128), 128)])
        panel_out[pl.ds(4 * i, 4), :, 0:128] = dot3(a, trail, nt).reshape(4, 32, 128)
        corner = jnp.concatenate([dot3(a, lead, nt), jnp.zeros((128, 96), F32)], axis=1)
        panel_out[pl.ds(4 * i, 4), :, 128:256] = corner.reshape(4, 32, 128)
        return carry

    lax.fori_loop(0, 4, panel, 0)


def kernel_gram(desc, points, weight):
    dma = pltpu.SemaphoreType.DMA
    vmem = pl.BlockSpec(memory_space=pltpu.VMEM)
    return pl.pallas_call(
        gather_and_multiply,
        out_shape=(jax.ShapeDtypeStruct((5, 256, 128), F32), jax.ShapeDtypeStruct((16, 32, 256), F32)),
        in_specs=[vmem] * 3,
        out_specs=[vmem] * 2,
        scratch_shapes=[
            pltpu.VMEM((80, 64), F32),
            pltpu.VMEM((8, 1024), F32),
            pltpu.VMEM((384, 128), F32),
            pltpu.VMEM((2, 2, 384, 1024), F32),
            pltpu.VMEM((16, 64, 1024), F32),
            pltpu.VMEM((1024, 1024), BF16),
            pltpu.VMEM((1024, 1024), BF16),
            pltpu.VMEM((320, 1024), BF16),
            pltpu.VMEM((320, 1024), BF16),
            pltpu.VMEM((512, 1024), F32),
            pltpu.VMEM((3, 256, 1024), F32),
            dma((3,)), dma((3,)), dma, dma, dma,
            dma((8,)), dma((8,)), dma((4,)), dma((4,)),
            dma((16,)), dma((16,)), dma((16,)), dma((16,)),
            dma((8,)), dma((8,)), dma((8,)), dma((8,)),
        ],
        compiler_params=pltpu.CompilerParams(collective_id=0, has_side_effects=True, vmem_limit_bytes=60 * 2**20),
    )(desc, points, weight)


def reduce_and_share(
    tt, pp, corner, p_rows, p_cols, block,
    p_in, tt_in, t_own, c_own, tt_own,
    p_s, p_r, tt_s, tt_r, col_s, col_r, row_s, row_r, cor_s, cor_r, blk_s, blk_r,
):
    e, p, x, y, z, c = placed()
    h = p // 8
    me = 4 * x + y
    barrier = pltpu.get_barrier_semaphore()

    def is_me(to):
        return (to[0] == e) & (to[1] == p)

    def greet(who):
        @pl.when(jnp.logical_not(is_me(who)))
        def _():
            pl.semaphore_signal(barrier, inc=1, device_id=who, device_id_type=MESH)

    def send(src, dst, send_sem, recv_sem, to, also=None):
        here, there = is_me(to), jnp.logical_not(is_me(to))
        if also is not None:
            here, there = here & also, there & also

        @pl.when(here)
        def _():
            pltpu.make_async_copy(src, dst, recv_sem).start()

        @pl.when(there)
        def _():
            remote(src, dst, send_sem, recv_sem, to).start()

        def finish():
            @pl.when(there)
            def _():
                remote(src, dst, send_sem, recv_sem, to).wait_send()

        return finish

    z_row, z_col = e % 8, z
    apart = (z_col + 8 - z_row) % 8
    straight = apart <= 4
    gap = jnp.where(straight, apart, 8 - apart)
    z_first = jnp.where(straight, z_row, z_col)
    h_first = jnp.where(straight, e // 8, h)
    h_second = jnp.where(straight, h, e // 8)
    z_from = (z_first + 8 - jnp.where(gap == 3, 1, 0)) % 8
    c_from = jnp.where(gap == 0, h_second, jnp.where(gap >= 3, 1, 0))

    for q in range(16):
        greet(device(q // 4, q % 4, z, h))
        greet(device(q // 4, q % 4, z, c))
        greet((q, p))
        greet((q, e))
    for t in range(8):
        q = 8 * h_first + t
        greet(device(q // 4, q % 4, z_from, c_from))

    owners = []
    for k in range(5):
        first = (k + 1) // 2
        d_row = c if first == 1 else 0
        d_col = (0, 1 + 3 * c, 2 + 2 * c)[first]
        side = c if k == 0 else (k + 1) % 2
        p_a = 8 * (me // 8) + (z + d_row) % 8
        p_b = 8 * side + (z + d_col) % 8
        owners.append((2 * k, k, (p_a, p_b), None))
        if k > 0:
            owners.append((2 * k + 1, k, (p_b, p_a), None if first == 1 else c == 0))

    targets = [(a, 8 * c + z) for a in range(16)] + [device(q // 4, q % 4, z, c) for q in range(16)]
    targets += [(p, q) for q in range(16)] + [(q, p) for q in range(16)]
    expected = 0
    for to in targets:
        expected = expected + jnp.where(is_me(to), 0, 1)
    for _, _, to, also in owners:
        counts = jnp.logical_not(is_me(to)) if also is None else jnp.logical_not(is_me(to)) & also
        expected = expected + jnp.where(counts, 1, 0)
    pl.semaphore_wait(barrier, expected)

    pending = []
    for a in range(16):
        pending.append(send(pp.at[a], p_in.at[me], p_s.at[a], p_r.at[me], (a, 8 * c + z)))
    for q in range(16):
        to = device(q // 4, q % 4, z, c)
        pending.append(send(tt.at[:, 16 * q : 16 * q + 16], tt_in.at[me], tt_s.at[q], tt_r.at[me], to))

    for q in range(16):
        arrived(p_in.at[q], p_r.at[q])
    total = p_in[0]
    for q in range(1, 16):
        total = total + p_in[q]
    at = lax.broadcasted_iota(jnp.int32, (32, 256), 1)
    one = (at == 128 + lax.broadcasted_iota(jnp.int32, (32, 256), 0)) & (e == p)
    t_own[...] = total + jnp.where(one, 1.0, 0.0)
    for q in range(16):
        pending.append(send(t_own, p_rows.at[e], row_s.at[q], row_r.at[e], (p, q)))
    for q in range(16):
        pending.append(send(t_own, p_cols.at[e], col_s.at[q], col_r.at[e], (q, p)))

    for q in range(16):
        arrived(p_rows.at[q], row_r.at[q])
    for q in range(4):
        strip = p_rows[4 * q : 4 * q + 4, :, 128:256].reshape(128, 128)
        c_own[:, 128 * q : 128 * q + 128] = jnp.transpose(strip)[0:32]
    for q in range(16):
        pending.append(send(c_own, corner.at[e], cor_s.at[q], cor_r.at[e], (q, p)))

    for q in range(16):
        arrived(tt_in.at[q], tt_r.at[q])
    total = tt_in[0]
    for q in range(1, 16):
        total = total + tt_in[q]
    tt_own[...] = total
    part = me % 8
    rows = pl.ds(pl.multiple_of(16 * part, 16), 16)
    for n, k, to, also in owners:
        pending.append(send(tt_own.at[k], block.at[rows], blk_s.at[n], blk_r.at[part], to, also))

    for q in range(16):
        arrived(p_cols.at[q], col_r.at[q])
        arrived(corner.at[q], cor_r.at[q])
    for t in range(8):
        arrived(block.at[16 * t : 16 * t + 16], blk_r.at[t])
    for finish in pending:
        finish()


def share(tt, pp):
    dma = pltpu.SemaphoreType.DMA
    vmem = pl.BlockSpec(memory_space=pltpu.VMEM)
    return pl.pallas_call(
        reduce_and_share,
        out_shape=(
            jax.ShapeDtypeStruct((16, 32, 512), F32),
            jax.ShapeDtypeStruct((16, 32, 256), F32),
            jax.ShapeDtypeStruct((16, 32, 256), F32),
            jax.ShapeDtypeStruct((128, 128), F32),
        ),
        in_specs=[vmem] * 2,
        out_specs=[vmem] * 4,
        scratch_shapes=[
            pltpu.VMEM((16, 32, 256), F32),
            pltpu.VMEM((16, 5, 16, 128), F32),
            pltpu.VMEM((32, 256), F32),
            pltpu.VMEM((32, 512), F32),
            pltpu.VMEM((5, 16, 128), F32),
        ]
        + [dma((16,))] * 12,
        compiler_params=pltpu.CompilerParams(collective_id=1, has_side_effects=True, vmem_limit_bytes=32 * 2**20),
    )(tt, pp)


def dot_hi(a, b, dims):
    return lax.dot_general(a, b, (dims, ((), ())), precision=HI, preferred_element_type=F32)


def inverse_factor(d_ref, e_ref):
    rows = lax.broadcasted_iota(jnp.int32, (8, NB), 0)
    lanes = lax.broadcasted_iota(jnp.int32, (8, NB), 1)
    groups = NB // 8
    full = lambda v: jnp.broadcast_to(v, (8, NB))
    for g in range(groups):
        e_ref[8 * g : 8 * g + 8, :] = (lanes == rows + 8 * g).astype(F32)
    for t in range(groups):
        v = d_ref[8 * t : 8 * t + 8, :]
        e = e_ref[8 * t : 8 * t + 8, :]
        c = [full(v[:, 8 * t + i : 8 * t + i + 1]) for i in range(8)]
        v_row, e_row, c_row, inv = [], [], [], []
        pivots = jnp.ones((8, NB), F32)
        for i in range(8):
            pivot = full(c[i][i : i + 1])
            pivots = jnp.where(rows == i, pivot, pivots)
            r = 1.0 / pivot
            inv.append(r)
            v_row.append(full(v[i : i + 1]))
            e_row.append(full(e[i : i + 1]))
            c_row.append([full(c[k][i : i + 1]) if k > i else None for k in range(8)])
            if i < 7:
                m = jnp.where(rows > i, c[i] * r, 0.0)
                for k in range(i + 1, 8):
                    c[k] = c[k] - m * c_row[i][k]
                v = v - m * v_row[i]
                e = e - m * e_row[i]
        e_ref[8 * t : 8 * t + 8, :] = e * lax.rsqrt(pivots)
        for g in range(t + 1, groups):
            v = d_ref[8 * g : 8 * g + 8, :]
            e = e_ref[8 * g : 8 * g + 8, :]
            c = [full(v[:, 8 * t + i : 8 * t + i + 1]) for i in range(8)]
            for i in range(8):
                m = c[i] * inv[i]
                for k in range(i + 1, 8):
                    c[k] = c[k] - m * c_row[i][k]
                v = v - m * v_row[i]
                e = e - m * e_row[i]
            d_ref[8 * g : 8 * g + 8, :] = v
            e_ref[8 * g : 8 * g + 8, :] = e


def factor_and_update(where, corner, p_rows, p_cols, block, panel_ref, trail_ref, a, ui, uj, d, inv_ref):
    e, p = where[0], where[1]
    n = a.shape[0]
    a[...] = corner[...].reshape(n, n)
    ui[...] = p_rows[...].reshape(n, 256)
    uj[...] = p_cols[:, :, 0:128].reshape(n, 128)
    for k in range(n // NB):
        lo, hi = k * NB, (k + 1) * NB
        d[...] = a[lo:hi, lo:hi]
        inverse_factor(d, inv_ref)
        inv = inv_ref[...]
        ui[lo:hi, :] = dot_hi(inv, ui[lo:hi, :], ((1,), (0,)))
        uj[lo:hi, :] = dot_hi(inv, uj[lo:hi, :], ((1,), (0,)))
        if hi < n:
            a[lo:hi, hi:] = dot_hi(inv, a[lo:hi, hi:], ((1,), (0,)))
            u = a[lo:hi, hi:]
            a[hi:, hi:] -= dot_hi(u, u, ((0,), (0,)))
            ui[hi:, :] -= dot_hi(u, ui[lo:hi, :], ((0,), (0,)))
            uj[hi:, :] -= dot_hi(u, uj[lo:hi, :], ((0,), (0,)))
    gram = block[...]
    straight = (p % 8 + 8 - e % 8) % 8 <= 4
    gram = jnp.where(straight, gram, jnp.transpose(gram))
    same = lax.broadcasted_iota(jnp.int32, (128, 128), 0) == lax.broadcasted_iota(jnp.int32, (128, 128), 1)
    gram = gram + jnp.where(same & (e == p), 1.0, 0.0)
    trail_ref[...] = gram - dot_hi(ui[:, 0:128], uj[...], ((0,), (0,)))
    strip = jnp.transpose(ui[pl.ds(pl.multiple_of(32 * p, 32), 32), :])
    panel_ref[0:32, :] = strip[128:160]
    panel_ref[32:160, :] = strip[0:128]


def factor(where, corner, p_rows, p_cols, block):
    vmem = pl.BlockSpec(memory_space=pltpu.VMEM)
    return pl.pallas_call(
        factor_and_update,
        out_shape=(jax.ShapeDtypeStruct((160, 32), F32), jax.ShapeDtypeStruct((128, 128), F32)),
        in_specs=[pl.BlockSpec(memory_space=pltpu.SMEM)] + [vmem] * 4,
        out_specs=[vmem] * 2,
        scratch_shapes=[
            pltpu.VMEM((512, 512), F32),
            pltpu.VMEM((512, 256), F32),
            pltpu.VMEM((512, 128), F32),
            pltpu.VMEM((NB, NB), F32),
            pltpu.VMEM((NB, NB), F32),
        ],
    )(where, corner, p_rows, p_cols, block)


def local(descriptors, env_weight, points):
    weight = jnp.broadcast_to(env_weight[None, :], (8, env_weight.shape[0]))
    tt, pp = kernel_gram(descriptors, points, weight)
    shared = share(tt, pp)
    where = jnp.stack([lax.axis_index("env"), lax.axis_index("pts")]).astype(jnp.int32)
    return factor(where, *shared)


def solution(mesh):
    return jax.shard_map(
        local,
        mesh=mesh,
        in_specs=(P("pts", "env"), P("env"), P("pts", "env")),
        out_specs=(P("env", "pts"), P("env", "pts")),
        check_vma=False,
    )
```

```python
import functools

import jax
import jax.numpy as jnp
from jax import lax
from jax.experimental import pallas as pl
from jax.experimental.pallas import tpu as pltpu
from jax.sharding import PartitionSpec as P

MESH = pl.DeviceIdType.MESH
HI = lax.Precision.HIGHEST
F32 = jnp.float32
BF16 = jnp.bfloat16
NB = 128
NENV = 16384
OFFSETS = (0, 1, 2, 4)


def placed():
    e, p = lax.axis_index("env"), lax.axis_index("pts")
    x, y_lo, c = e // 4, (e // 2) % 2, e % 2
    y_hi, z = p // 8, p % 8
    return e, p, x, 2 * y_hi + y_lo, z, c


def device(x, y, z, c):
    return (4 * x + 2 * (y % 2) + c, 8 * (y // 2) + z)


def remote(src, dst, send_sem, recv_sem, to):
    return pltpu.make_async_remote_copy(
        src_ref=src, dst_ref=dst, send_sem=send_sem, recv_sem=recv_sem, device_id=to, device_id_type=MESH
    )


def arrived(ref, sem):
    pltpu.make_async_copy(ref, ref, sem).wait()


def halves(a):
    hi = a.astype(BF16)
    return hi, (a - hi.astype(F32)).astype(BF16)


def dot3(a, b, dims):
    one = lambda l, r: lax.dot_general(l, r, (dims, ((), ())), preferred_element_type=F32)
    return one(a[0], b[0]) + (one(a[0], b[1]) + one(a[1], b[0]))


def gather_and_multiply(
    desc, points, weight, tt_out, panel_out, corner_out,
    half, other_weight, line, table, feats, feats_hi, feats_lo, rows_hi, rows_lo, kp, kt,
    half_s, half_r, swap_s, swap_r, local_s, zp_s, zp_r, zt_s, zt_r, slab_s, slab_r, slabx_s, slabx_r,
    ring_s, ring_r, ringx_s, ringx_r,
):
    e, p, x, y, z, c = placed()
    h = p // 8
    native = c == h
    turn = jnp.where(native, 1, 7)
    sibling = device(x, y, z, 1 - c)
    partner = device(x, (y + 2) % 4, z, 1 - c)
    along_z = lambda d: device(x, y, (z + d) % 8, c)

    def step(j1, j2):
        return (x + j1 * (1 - c) + j2 * c) % 4, (y + j1 * c + j2 * (1 - c)) % 4

    def slab_of(j1, j2, core):
        sx = (x + 8 - j1 * (1 - core) - j2 * core) % 4
        sy = (y + 8 - j1 * core - j2 * (1 - core)) % 4
        lanes = pl.multiple_of(128 * (2 * sx + sy % 2), 128)
        return table.at[sy // 2, core, :, pl.ds(lanes, 128)]

    barrier = pltpu.get_barrier_semaphore()
    greet = [sibling, partner] + [along_z(d) for d in range(1, 8)]
    greet += [device(*step(j, 0), z, c) for j in (1, 2, 3)] + [device(*step(0, j), z, c) for j in (1, 2, 3)]
    for who in greet:
        pl.semaphore_signal(barrier, inc=1, device_id=who, device_id_type=MESH)
    pl.semaphore_wait(barrier, len(greet))

    o = 1 - c
    to_sibling = [
        remote(points.at[pl.ds(pl.multiple_of(16 * o, 16), 16)], half.at[0:16], half_s.at[0], half_r.at[0], sibling),
        remote(points.at[pl.ds(pl.multiple_of(32 + 64 * o, 32), 64)], half.at[16:80], half_s.at[1], half_r.at[1], sibling),
        remote(weight, other_weight, half_s.at[2], half_r.at[2], sibling),
    ]
    for copy in to_sibling:
        copy.start()
    swap = remote(desc, feats.at[p], swap_s, swap_r, partner)
    keep = pltpu.make_async_copy(desc, feats.at[p], swap_r)

    @pl.when(native)
    def _():
        keep.start()

    @pl.when(jnp.logical_not(native))
    def _():
        swap.start()

    arrived(half.at[0:16], half_r.at[0])
    arrived(half.at[16:80], half_r.at[1])
    mine = jnp.concatenate(
        [points[pl.ds(pl.multiple_of(16 * c, 16), 16)], points[pl.ds(pl.multiple_of(32 + 64 * c, 32), 64)]], axis=0
    )
    theirs = half[...]
    packed = jnp.where(c == 0, jnp.concatenate([mine, theirs], axis=1), jnp.concatenate([theirs, mine], axis=1))
    own_panel = line.at[pl.ds(pl.multiple_of(16 * z, 16), 16)]
    line[pl.ds(pl.multiple_of(16 * z, 16), 16)] = packed[0:16]
    line[128:192] = packed[16:80]

    lined = []
    for s in (1, 2, 3):
        rows = pl.ds(128 + 64 * s, 64)
        lined.append(remote(line.at[128:192], line.at[rows], zt_s.at[s], zt_r.at[s], along_z(8 - OFFSETS[s])))
    for d in range(1, 8):
        lined.append(remote(own_panel, own_panel, zp_s.at[d], zp_r.at[d], along_z(d)))
    for copy in lined:
        copy.start()

    def piece(m, core, sign):
        d = (0, 1, 2, 3, 4, 7, 6, 5)[m]
        return feats.at[8 * core + (z + 8 * 8 - sign * d) % 8]

    rings, across = [], []

    def pass_on(m):
        src = piece(m, c, turn)
        if m in (0, 1, 2, 3):
            copy = remote(src, src, ring_s.at[m + 1], ring_r.at[m + 1], along_z(turn))
            copy.start()
            rings.append(copy)
        if m in (0, 5, 6):
            n = 5 if m == 0 else m + 1
            copy = remote(src, src, ring_s.at[n], ring_r.at[n], along_z(8 - turn))
            copy.start()
            rings.append(copy)
        copy = remote(src, src, ringx_s.at[m], ringx_r.at[m], sibling)
        copy.start()
        across.append(copy)

    arrived(piece(0, c, turn), swap_r)
    pass_on(0)

    for s in (1, 2, 3):
        arrived(line.at[pl.ds(128 + 64 * s, 64)], zt_r.at[s])
    for d in range(1, 8):
        rows = pl.ds(pl.multiple_of(16 * ((z + 8 - d) % 8), 16), 16)
        arrived(line.at[rows], zp_r.at[d])

    slabs = []

    def spread(j1, src, dst):
        if j1 == 0:
            for j in (1, 2, 3):
                slabs.append(remote(src, dst, slab_s.at[4 * j], slab_r.at[4 * j], device(*step(j, 0), z, c)))
                slabs[-1].start()
        for j in (1, 2, 3):
            n = 4 * j1 + j
            slabs.append(remote(src, dst, slab_s.at[n], slab_r.at[n], device(*step(0, j), z, c)))
            slabs[-1].start()

    def to_other_core(n, src, dst):
        slabs.append(remote(src, dst, slabx_s.at[n], slabx_r.at[n], sibling))
        slabs[-1].start()

    own = slab_of(0, 0, c)
    spread(0, line, own)
    to_other_core(0, line, own)
    stay = pltpu.make_async_copy(line, own, local_s)
    stay.start()

    def take_piece(m):
        arrived(piece(m, c, turn), ring_r.at[m])
        pass_on(m)

    def take_slab(j1, j2):
        here = slab_of(j1, j2, c)
        arrived(here, slab_r.at[4 * j1 + j2])
        if j2 == 0:
            spread(j1, here, here)
        to_other_core(4 * j1 + j2, here, here)

    take_slab(1, 0)
    take_slab(3, 0)
    take_piece(1)
    take_piece(5)
    take_slab(2, 0)
    take_slab(0, 1)
    take_slab(0, 3)
    take_slab(0, 2)
    take_piece(2)
    take_piece(6)
    for j1 in (1, 3):
        for j2 in (1, 3, 2):
            take_slab(j1, j2)
    take_piece(3)
    take_piece(7)
    for j2 in (1, 3, 2):
        take_slab(2, j2)
    take_piece(4)

    for m in range(8):
        arrived(piece(m, o, 8 - turn), ringx_r.at[m])
    for j1 in range(4):
        for j2 in range(4):
            arrived(slab_of(j1, j2, o), slabx_r.at[4 * j1 + j2])
    stay.wait()
    arrived(other_weight, half_r.at[2])
    for copy in to_sibling + lined + rings + across + slabs:
        copy.wait_send()

    @pl.when(jnp.logical_not(native))
    def _():
        swap.wait_send()

    def split_feats(i, carry):
        hi, lo = halves(feats[i])
        rows = pl.ds(pl.multiple_of(64 * i, 64), 64)
        feats_hi[rows] = hi
        feats_lo[rows] = lo
        return carry

    lax.fori_loop(0, 16, split_feats, 0)

    def kernel_rows(i, carry):
        hh, cc = i // 2, i % 2
        hi, lo = halves(table[hh, cc, 0:256])
        rows_hi[0:256], rows_lo[0:256] = hi, lo
        hi, lo = halves(table[hh, cc, pl.ds(pl.multiple_of(256 + 64 * c, 64), 64)])
        rows_hi[256:320], rows_lo[256:320] = hi, lo

        def columns(t, carry):
            lanes = pl.ds(pl.multiple_of(256 * t, 256), 256)
            scaled = dot3(
                (rows_hi[...], rows_lo[...]), (feats_hi[:, lanes], feats_lo[:, lanes]), ((1,), (0,))
            ) * (1.0 / 32.0)
            value = 0.25 * scaled * scaled * scaled
            for zz in range(8):
                at = pl.multiple_of(256 * hh + 32 * zz + 16 * cc, 16)
                kp[pl.ds(at, 16), lanes] = value[16 * zz : 16 * zz + 16]
            for s in range(3):
                at = pl.multiple_of(128 * hh + 64 * cc, 64)
                kt[s, pl.ds(at, 64), lanes] = value[128 + 64 * s : 192 + 64 * s]
            return carry

        lax.fori_loop(0, 4, columns, 0)
        return carry

    lax.fori_loop(0, 4, kernel_rows, 0)

    w = jnp.where(native, weight[0:1], other_weight[0:1]) * (1.0 / NENV)
    nt = ((1,), (1,))

    def unit(k, carry):
        first = (k + 1) // 2
        row = jnp.where(first == 1, c, 0)
        col = jnp.where(first == 0, 0, jnp.where(first == 1, 1 + c, 2))
        side = jnp.where(first == 0, c, (k + 1) % 2)
        a = halves(kt[row] * w)
        b = halves(kt[col, pl.ds(pl.multiple_of(128 * side, 128), 128)])
        tt_out[k] = dot3(a, b, nt)
        return carry

    lax.fori_loop(0, 5, unit, 0)
    trail = halves(kt[0, pl.ds(pl.multiple_of(128 * c, 128), 128)] * w)
    lead = halves(kp[pl.ds(pl.multiple_of(256 * c + 32 * z, 32), 32)] * w)

    def panel(i, carry):
        a = halves(kp[pl.ds(pl.multiple_of(128 * i, 128), 128)])
        panel_out[pl.ds(4 * i, 4)] = dot3(a, trail, nt).reshape(4, 32, 128)
        corner_out[i] = dot3(lead, a, nt)
        return carry

    lax.fori_loop(0, 4, panel, 0)


def kernel_gram(desc, points, weight):
    dma = pltpu.SemaphoreType.DMA
    vmem = pl.BlockSpec(memory_space=pltpu.VMEM)
    return pl.pallas_call(
        gather_and_multiply,
        out_shape=(
            jax.ShapeDtypeStruct((5, 256, 128), F32),
            jax.ShapeDtypeStruct((16, 32, 128), F32),
            jax.ShapeDtypeStruct((4, 32, 128), F32),
        ),
        in_specs=[vmem] * 3,
        out_specs=[vmem] * 3,
        scratch_shapes=[
            pltpu.VMEM((80, 64), F32),
            pltpu.VMEM((8, 1024), F32),
            pltpu.VMEM((384, 128), F32),
            pltpu.VMEM((2, 2, 384, 1024), F32),
            pltpu.VMEM((16, 64, 1024), F32),
            pltpu.VMEM((1024, 1024), BF16),
            pltpu.VMEM((1024, 1024), BF16),
            pltpu.VMEM((320, 1024), BF16),
            pltpu.VMEM((320, 1024), BF16),
            pltpu.VMEM((512, 1024), F32),
            pltpu.VMEM((3, 256, 1024), F32),
            dma((3,)), dma((3,)), dma, dma, dma,
            dma((8,)), dma((8,)), dma((4,)), dma((4,)),
            dma((16,)), dma((16,)), dma((16,)), dma((16,)),
            dma((8,)), dma((8,)), dma((8,)), dma((8,)),
        ],
        compiler_params=pltpu.CompilerParams(collective_id=0, has_side_effects=True, vmem_limit_bytes=60 * 2**20),
    )(desc, points, weight)


def dot_hi(a, b, dims):
    return lax.dot_general(a, b, (dims, ((), ())), precision=HI, preferred_element_type=F32)


def inverse_factor(d_ref, e_ref):
    rows = lax.broadcasted_iota(jnp.int32, (8, NB), 0)
    lanes = lax.broadcasted_iota(jnp.int32, (8, NB), 1)
    groups = NB // 8
    full = lambda v: jnp.broadcast_to(v, (8, NB))
    for g in range(groups):
        e_ref[8 * g : 8 * g + 8, :] = (lanes == rows + 8 * g).astype(F32)
    for t in range(groups):
        v = d_ref[8 * t : 8 * t + 8, :]
        e = e_ref[8 * t : 8 * t + 8, :]
        c = [full(v[:, 8 * t + i : 8 * t + i + 1]) for i in range(8)]
        v_row, e_row, c_row, inv = [], [], [], []
        pivots = jnp.ones((8, NB), F32)
        for i in range(8):
            pivot = full(c[i][i : i + 1])
            pivots = jnp.where(rows == i, pivot, pivots)
            r = 1.0 / pivot
            inv.append(r)
            v_row.append(full(v[i : i + 1]))
            e_row.append(full(e[i : i + 1]))
            c_row.append([full(c[k][i : i + 1]) if k > i else None for k in range(8)])
            if i < 7:
                m = jnp.where(rows > i, c[i] * r, 0.0)
                for k in range(i + 1, 8):
                    c[k] = c[k] - m * c_row[i][k]
                v = v - m * v_row[i]
                e = e - m * e_row[i]
        e_ref[8 * t : 8 * t + 8, :] = e * lax.rsqrt(pivots)
        for g in range(t + 1, groups):
            v = d_ref[8 * g : 8 * g + 8, :]
            e = e_ref[8 * g : 8 * g + 8, :]
            c = [full(v[:, 8 * t + i : 8 * t + i + 1]) for i in range(8)]
            for i in range(8):
                m = c[i] * inv[i]
                for k in range(i + 1, 8):
                    c[k] = c[k] - m * c_row[i][k]
                v = v - m * v_row[i]
                e = e - m * e_row[i]
            d_ref[8 * g : 8 * g + 8, :] = v
            e_ref[8 * g : 8 * g + 8, :] = e


def finish_panel(
    tt, pp, cc, panel_ref, trail_ref,
    c_in, c_z, c_all, p_in, p_rows, p_cols, t_own, tt_in, tt_own, block, a, ui, uj, d, inv_ref, strip,
    c_s, c_r, cz_s, cz_r, cp_s, cp_r, cx_s, cx_r, keep_s,
    p_s, p_r, tt_s, tt_r, col_s, col_r, row_s, row_r, blk_s, blk_r,
):
    e, p, x, y, z, c = placed()
    h = p // 8
    me = 4 * x + y
    sibling = device(x, y, z, 1 - c)
    in_plane = lambda q: device((x + q // 4) % 4, (y + q % 4) % 4, z, c)
    index_at = lambda q: 4 * ((x + q // 4) % 4) + (y + q % 4) % 4
    index_from = lambda q: 4 * ((x + 4 - q // 4) % 4) + (y + 4 - q % 4) % 4
    along_z = lambda q: device(x, y, (z + q) % 8, c)
    barrier = pltpu.get_barrier_semaphore()

    def is_me(to):
        return (to[0] == e) & (to[1] == p)

    def greet(who):
        @pl.when(jnp.logical_not(is_me(who)))
        def _():
            pl.semaphore_signal(barrier, inc=1, device_id=who, device_id_type=MESH)

    def send(src, dst, send_sem, recv_sem, to, also=None):
        here, there = is_me(to), jnp.logical_not(is_me(to))
        if also is not None:
            here, there = here & also, there & also

        @pl.when(here)
        def _():
            pltpu.make_async_copy(src, dst, recv_sem).start()

        @pl.when(there)
        def _():
            remote(src, dst, send_sem, recv_sem, to).start()

        def finish():
            @pl.when(there)
            def _():
                remote(src, dst, send_sem, recv_sem, to).wait_send()

        return finish

    z_row, z_col = e % 8, z
    apart = (z_col + 8 - z_row) % 8
    straight = apart <= 4
    gap = jnp.where(straight, apart, 8 - apart)
    z_first = jnp.where(straight, z_row, z_col)
    h_first = jnp.where(straight, e // 8, h)
    h_second = jnp.where(straight, h, e // 8)
    z_from = (z_first + 8 - jnp.where(gap == 3, 1, 0)) % 8
    c_from = jnp.where(gap == 0, h_second, jnp.where(gap >= 3, 1, 0))

    owners = []
    for k in range(5):
        first = (k + 1) // 2
        d_row = c if first == 1 else 0
        d_col = (0, 1 + 3 * c, 2 + 2 * c)[first]
        side = c if k == 0 else (k + 1) % 2
        p_a = 8 * (me // 8) + (z + d_row) % 8
        p_b = 8 * side + (z + d_col) % 8
        owners.append((2 * k, k, (p_a, p_b), None))
        if k > 0:
            owners.append((2 * k + 1, k, (p_b, p_a), None if first == 1 else c == 0))

    pl.semaphore_signal(barrier, inc=1, device_id=sibling, device_id_type=MESH)
    for q in range(1, 16):
        pl.semaphore_signal(barrier, inc=1, device_id=in_plane(q), device_id_type=MESH)
    for q in range(1, 8):
        pl.semaphore_signal(barrier, inc=1, device_id=along_z(q), device_id_type=MESH)
    for q in range(16):
        greet(device(q // 4, q % 4, z, h))
        greet((q, p))
        greet((q, e))
    for t in range(8):
        q = 8 * h_first + t
        greet(device(q // 4, q % 4, z_from, c_from))
    targets = [(q, 8 * c + z) for q in range(16)] + [(p, q) for q in range(16)] + [(q, p) for q in range(16)]
    expected = 23
    for to in targets:
        expected = expected + jnp.where(is_me(to), 0, 1)
    for _, _, to, also in owners:
        counts = jnp.logical_not(is_me(to)) if also is None else jnp.logical_not(is_me(to)) & also
        expected = expected + jnp.where(counts, 1, 0)
    pl.semaphore_wait(barrier, expected)

    pending, plain = [], []

    def go(copy):
        copy.start()
        plain.append(copy)

    def corner_rows(q):
        return pl.ds(pl.multiple_of(8 * (q // 4), 8), 8)

    stay = pltpu.make_async_copy(cc.at[me % 4, corner_rows(me)], c_in.at[me], c_r.at[0])
    stay.start()
    for q in range(1, 16):
        there = index_at(q)
        go(remote(cc.at[there % 4, corner_rows(there)], c_in.at[me], c_s.at[q], c_r.at[q], in_plane(q)))
    for q in range(16):
        pending.append(send(pp.at[q], p_in.at[me], p_s.at[q], p_r.at[me], (q, 8 * c + z)))

    for q in range(16):
        arrived(c_in.at[index_from(q)], c_r.at[q])
    total = c_in[0]
    for q in range(1, 16):
        total = total + c_in[q]
    at_row = 256 * c + 32 * z + 8 * (me // 4) + lax.broadcasted_iota(jnp.int32, (8, 128), 0)
    at_col = 128 * (me % 4) + lax.broadcasted_iota(jnp.int32, (8, 128), 1)
    c_z[z] = total + jnp.where(at_row == at_col, 1.0, 0.0)
    for q in range(1, 8):
        go(remote(c_z.at[z], c_z.at[z], cz_s.at[q], cz_r.at[q], along_z(q)))
    for q in range(1, 8):
        arrived(c_z.at[(z + 8 - q) % 8], cz_r.at[q])

    def corner_part(q, core):
        return c_all.at[core, :, q // 4, :, pl.ds(pl.multiple_of(128 * (q % 4), 128), 128)]

    for q in range(1, 16):
        go(remote(c_z, corner_part(me, c), cp_s.at[q], cp_r.at[q], in_plane(q)))
    go(remote(c_z, corner_part(me, c), cx_s.at[0], cx_r.at[0], sibling))
    keep = pltpu.make_async_copy(c_z, corner_part(me, c), keep_s)
    keep.start()

    for q in range(16):
        arrived(p_in.at[q], p_r.at[q])
    total = p_in[0]
    for q in range(1, 16):
        total = total + p_in[q]
    t_own[...] = total
    for q in range(16):
        pending.append(send(t_own, p_rows.at[e], row_s.at[q], row_r.at[e], (p, q)))
        pending.append(send(t_own, p_cols.at[e], col_s.at[q], col_r.at[e], (q, p)))

    for q in range(1, 16):
        part = corner_part(index_from(q), c)
        arrived(part, cp_r.at[q])
        go(remote(part, part, cx_s.at[q], cx_r.at[q], sibling))
    for q in range(16):
        go_to = device(q // 4, q % 4, z, c)
        pending.append(send(tt.at[:, 16 * q : 16 * q + 16], tt_in.at[me], tt_s.at[q], tt_r.at[me], go_to))
    keep.wait()
    for q in range(16):
        arrived(corner_part(index_from(q), 1 - c), cx_r.at[q])

    n = a.shape[0]
    a[...] = c_all[...].reshape(n, n)
    ui[:, 128:256] = a[:, pl.ds(pl.multiple_of(128 * (e // 4), 128), 128)]
    for k in range(n // NB):
        lo, hi = k * NB, (k + 1) * NB
        d[...] = a[lo:hi, lo:hi]
        inverse_factor(d, inv_ref)
        inv = inv_ref[...]
        if hi < n:
            a[lo:hi, hi:] = dot_hi(inv, a[lo:hi, hi:], ((1,), (0,)))
            u = a[lo:hi, hi:]
            a[hi:, hi:] -= dot_hi(u, u, ((0,), (0,)))
        if k == 0:
            for q in range(16):
                arrived(tt_in.at[q], tt_r.at[q])
            total = tt_in[0]
            for q in range(1, 16):
                total = total + tt_in[q]
            tt_own[...] = total
            part = me % 8
            rows = pl.ds(pl.multiple_of(16 * part, 16), 16)
            for m, kk, to, also in owners:
                pending.append(send(tt_own.at[kk], block.at[rows], blk_s.at[m], blk_r.at[part], to, also))
            for q in range(16):
                arrived(p_rows.at[q], row_r.at[q])
                arrived(p_cols.at[q], col_r.at[q])
            ui[:, 0:128] = p_rows[...].reshape(n, 128)
            uj[...] = p_cols[...].reshape(n, 128)
        ui[lo:hi, :] = dot_hi(inv, ui[lo:hi, :], ((1,), (0,)))
        uj[lo:hi, :] = dot_hi(inv, uj[lo:hi, :], ((1,), (0,)))
        if hi < n:
            ui[hi:, :] -= dot_hi(u, ui[lo:hi, :], ((0,), (0,)))
            uj[hi:, :] -= dot_hi(u, uj[lo:hi, :], ((0,), (0,)))
    for t in range(8):
        arrived(block.at[16 * t : 16 * t + 16], blk_r.at[t])
    gram = block[...]
    gram = jnp.where(straight, gram, jnp.transpose(gram))
    same = lax.broadcasted_iota(jnp.int32, (128, 128), 0) == lax.broadcasted_iota(jnp.int32, (128, 128), 1)
    gram = gram + jnp.where(same & (e == p), 1.0, 0.0)
    trail_ref[...] = gram - dot_hi(ui[:, 0:128], uj[...], ((0,), (0,)))
    across = jnp.transpose(ui[pl.ds(pl.multiple_of(32 * p, 32), 32), :])
    strip[...] = across[128:256]
    panel_ref[0:32, :] = strip[pl.ds(pl.multiple_of(32 * (e % 4), 32), 32), :]
    panel_ref[32:160, :] = across[0:128]
    for copy in plain:
        copy.wait_send()
    for finish in pending:
        finish()


def finish(tt, pp, cc):
    dma = pltpu.SemaphoreType.DMA
    vmem = pl.BlockSpec(memory_space=pltpu.VMEM)
    return pl.pallas_call(
        finish_panel,
        out_shape=(jax.ShapeDtypeStruct((160, 32), F32), jax.ShapeDtypeStruct((128, 128), F32)),
        in_specs=[vmem] * 3,
        out_specs=[vmem] * 2,
        scratch_shapes=[
            pltpu.VMEM((16, 8, 128), F32),
            pltpu.VMEM((8, 8, 128), F32),
            pltpu.VMEM((2, 8, 4, 8, 512), F32),
            pltpu.VMEM((16, 32, 128), F32),
            pltpu.VMEM((16, 32, 128), F32),
            pltpu.VMEM((16, 32, 128), F32),
            pltpu.VMEM((32, 128), F32),
            pltpu.VMEM((16, 5, 16, 128), F32),
            pltpu.VMEM((5, 16, 128), F32),
            pltpu.VMEM((128, 128), F32),
            pltpu.VMEM((512, 512), F32),
            pltpu.VMEM((512, 256), F32),
            pltpu.VMEM((512, 128), F32),
            pltpu.VMEM((NB, NB), F32),
            pltpu.VMEM((NB, NB), F32),
            pltpu.VMEM((128, 32), F32),
        ]
        + [dma((16,))] * 8
        + [dma]
        + [dma((16,))] * 10,
        compiler_params=pltpu.CompilerParams(collective_id=1, has_side_effects=True, vmem_limit_bytes=32 * 2**20),
    )(tt, pp, cc)


def local(descriptors, env_weight, points):
    weight = jnp.broadcast_to(env_weight[None, :], (8, env_weight.shape[0]))
    return finish(*kernel_gram(descriptors, points, weight))


def solution(mesh):
    return jax.shard_map(
        local,
        mesh=mesh,
        in_specs=(P("pts", "env"), P("env"), P("pts", "env")),
        out_specs=(P("env", "pts"), P("env", "pts")),
        check_vma=False,
    )
```

```python
import functools

import jax
import jax.numpy as jnp
from jax import lax
from jax.experimental import pallas as pl
from jax.experimental.pallas import tpu as pltpu
from jax.sharding import PartitionSpec as P

MESH = pl.DeviceIdType.MESH
HI = lax.Precision.HIGHEST
F32 = jnp.float32
BF16 = jnp.bfloat16
NB = 128
NENV = 16384
OFFSETS = (0, 1, 2, 4)


def placed():
    e, p = lax.axis_index("env"), lax.axis_index("pts")
    x, y_lo, c = e // 4, (e // 2) % 2, e % 2
    y_hi, z = p // 8, p % 8
    return e, p, x, 2 * y_hi + y_lo, z, c


def device(x, y, z, c):
    return (4 * x + 2 * (y % 2) + c, 8 * (y // 2) + z)


def remote(src, dst, send_sem, recv_sem, to):
    return pltpu.make_async_remote_copy(
        src_ref=src, dst_ref=dst, send_sem=send_sem, recv_sem=recv_sem, device_id=to, device_id_type=MESH
    )


def arrived(ref, sem):
    pltpu.make_async_copy(ref, ref, sem).wait()


def halves(a):
    hi = a.astype(BF16)
    return hi, (a - hi.astype(F32)).astype(BF16)


def dot3(a, b, dims):
    one = lambda l, r: lax.dot_general(l, r, (dims, ((), ())), preferred_element_type=F32)
    return one(a[0], b[0]) + (one(a[0], b[1]) + one(a[1], b[0]))


def gather(
    spots, desc, points, weight,
    half, other_weight, line, table, feats,
    half_s, half_r, swap_s, swap_r, local_s, zp_s, zp_r, zt_s, zt_r, slab_s, slab_r, slabx_s, slabx_r,
    ring_s, ring_r, ringx_s, ringx_r,
):
    e, p, x, y, z, c = spots
    h = p // 8
    native = c == h
    turn = jnp.where(native, 1, 7)
    sibling = device(x, y, z, 1 - c)
    partner = device(x, (y + 2) % 4, z, 1 - c)
    along_z = lambda d: device(x, y, (z + d) % 8, c)

    def step(j1, j2):
        return (x + j1 * (1 - c) + j2 * c) % 4, (y + j1 * c + j2 * (1 - c)) % 4

    def slab_of(j1, j2, core):
        sx = (x + 8 - j1 * (1 - core) - j2 * core) % 4
        sy = (y + 8 - j1 * core - j2 * (1 - core)) % 4
        lanes = pl.multiple_of(128 * (2 * sx + sy % 2), 128)
        return table.at[sy // 2, core, :, pl.ds(lanes, 128)]

    o = 1 - c
    to_sibling = [
        remote(points.at[pl.ds(pl.multiple_of(16 * o, 16), 16)], half.at[0:16], half_s.at[0], half_r.at[0], sibling),
        remote(points.at[pl.ds(pl.multiple_of(32 + 64 * o, 32), 64)], half.at[16:80], half_s.at[1], half_r.at[1], sibling),
        remote(weight, other_weight, half_s.at[2], half_r.at[2], sibling),
    ]
    for copy in to_sibling:
        copy.start()
    parts = [pl.ds(32 * n, 32) for n in range(2)]
    swap = [remote(desc.at[r], feats.at[p, r], swap_s.at[n], swap_r.at[n], partner) for n, r in enumerate(parts)]
    keep = [pltpu.make_async_copy(desc.at[r], feats.at[p, r], swap_r.at[n]) for n, r in enumerate(parts)]

    @pl.when(native)
    def _():
        for copy in keep:
            copy.start()

    @pl.when(jnp.logical_not(native))
    def _():
        for copy in swap:
            copy.start()

    arrived(half.at[0:16], half_r.at[0])
    arrived(half.at[16:80], half_r.at[1])
    mine = jnp.concatenate(
        [points[pl.ds(pl.multiple_of(16 * c, 16), 16)], points[pl.ds(pl.multiple_of(32 + 64 * c, 32), 64)]], axis=0
    )
    theirs = half[...]
    packed = jnp.where(c == 0, jnp.concatenate([mine, theirs], axis=1), jnp.concatenate([theirs, mine], axis=1))
    own_panel = line.at[pl.ds(pl.multiple_of(16 * z, 16), 16)]
    line[pl.ds(pl.multiple_of(16 * z, 16), 16)] = packed[0:16]
    line[128:192] = packed[16:80]

    lined = []
    for s in (1, 2, 3):
        rows = pl.ds(128 + 64 * s, 64)
        lined.append(remote(line.at[128:192], line.at[rows], zt_s.at[s], zt_r.at[s], along_z(8 - OFFSETS[s])))
    for d in range(1, 8):
        lined.append(remote(own_panel, own_panel, zp_s.at[d], zp_r.at[d], along_z(d)))
    for copy in lined:
        copy.start()

    def piece(m, n, core, sign):
        d = (0, 1, 2, 3, 4, 7, 6, 5)[m]
        return feats.at[8 * core + (z + 8 * 8 - sign * d) % 8, parts[n]]

    rings, across = [], []

    def pass_on(m, n):
        src = piece(m, n, c, turn)
        if m in (0, 1, 2, 3):
            at = 2 * (m + 1) + n
            rings.append(remote(src, src, ring_s.at[at], ring_r.at[at], along_z(turn)))
            rings[-1].start()
        if m in (0, 5, 6):
            at = 2 * (5 if m == 0 else m + 1) + n
            rings.append(remote(src, src, ring_s.at[at], ring_r.at[at], along_z(8 - turn)))
            rings[-1].start()
        at = 2 * m + n
        across.append(remote(src, src, ringx_s.at[at], ringx_r.at[at], sibling))
        across[-1].start()

    for n in range(2):
        arrived(piece(0, n, c, turn), swap_r.at[n])
        pass_on(0, n)

    for s in (1, 2, 3):
        arrived(line.at[pl.ds(128 + 64 * s, 64)], zt_r.at[s])
    for d in range(1, 8):
        rows = pl.ds(pl.multiple_of(16 * ((z + 8 - d) % 8), 16), 16)
        arrived(line.at[rows], zp_r.at[d])

    slabs = []

    def forward(src, dst, j1, j2, to):
        n = 4 * j1 + j2
        slabs.append(remote(src, dst, slab_s.at[n], slab_r.at[n], device(*to, z, c)))
        slabs[-1].start()

    def to_other_core(n, src, dst):
        slabs.append(remote(src, dst, slabx_s.at[n], slabx_r.at[n], sibling))
        slabs[-1].start()

    own = slab_of(0, 0, c)
    forward(line, own, 1, 0, step(1, 0))
    forward(line, own, 3, 0, step(3, 0))
    forward(line, own, 0, 1, step(0, 1))
    forward(line, own, 0, 3, step(0, 3))
    to_other_core(0, line, own)
    stay = pltpu.make_async_copy(line, own, local_s)
    stay.start()

    def take_piece(m):
        for n in range(2):
            arrived(piece(m, n, c, turn), ring_r.at[2 * m + n])
            pass_on(m, n)

    def take_slab(j1, j2):
        here = slab_of(j1, j2, c)
        arrived(here, slab_r.at[4 * j1 + j2])
        if j2 == 0:
            if j1 == 1:
                forward(here, here, 2, 0, step(1, 0))
            forward(here, here, j1, 1, step(0, 1))
            forward(here, here, j1, 3, step(0, 3))
        if j2 == 1 and j1 in (0, 1):
            forward(here, here, j1, 2, step(0, 1))
        if j2 == 3 and j1 in (2, 3):
            forward(here, here, j1, 2, step(0, 3))
        to_other_core(4 * j1 + j2, here, here)

    take_slab(1, 0)
    take_slab(3, 0)
    take_piece(1)
    take_piece(5)
    take_slab(0, 1)
    take_slab(0, 3)
    take_slab(2, 0)
    take_slab(1, 1)
    take_slab(3, 3)
    take_piece(2)
    take_piece(6)
    take_slab(1, 3)
    take_slab(3, 1)
    take_slab(2, 3)
    take_slab(2, 1)
    take_slab(0, 2)
    take_piece(3)
    take_piece(7)
    take_slab(1, 2)
    take_slab(3, 2)
    take_slab(2, 2)
    take_piece(4)

    for m in range(8):
        for n in range(2):
            arrived(piece(m, n, o, 8 - turn), ringx_r.at[2 * m + n])
    for j1 in range(4):
        for j2 in range(4):
            arrived(slab_of(j1, j2, o), slabx_r.at[4 * j1 + j2])
    stay.wait()
    arrived(other_weight, half_r.at[2])

    def drain():
        for copy in to_sibling + lined + rings + across + slabs:
            copy.wait_send()

        @pl.when(jnp.logical_not(native))
        def _():
            for copy in swap:
                copy.wait_send()

    return drain


def kernel_values(spots, table, feats, feats_hi, feats_lo, rows_hi, rows_lo, kp, kt):
    c = spots[-1]

    def split_feats(i, carry):
        hi, lo = halves(feats[i])
        rows = pl.ds(pl.multiple_of(64 * i, 64), 64)
        feats_hi[rows] = hi
        feats_lo[rows] = lo
        return carry

    lax.fori_loop(0, 16, split_feats, 0)

    def kernel_rows(i, carry):
        hh, cc = i // 2, i % 2
        hi, lo = halves(table[hh, cc, 0:256])
        rows_hi[0:256], rows_lo[0:256] = hi, lo
        hi, lo = halves(table[hh, cc, pl.ds(pl.multiple_of(256 + 64 * c, 64), 64)])
        rows_hi[256:320], rows_lo[256:320] = hi, lo

        def columns(t, carry):
            lanes = pl.ds(pl.multiple_of(256 * t, 256), 256)
            scaled = dot3(
                (rows_hi[...], rows_lo[...]), (feats_hi[:, lanes], feats_lo[:, lanes]), ((1,), (0,))
            ) * (1.0 / 32.0)
            value = 0.25 * scaled * scaled * scaled
            for zz in range(8):
                at = pl.multiple_of(256 * hh + 32 * zz + 16 * cc, 16)
                kp[pl.ds(at, 16), lanes] = value[16 * zz : 16 * zz + 16]
            for s in range(3):
                at = pl.multiple_of(128 * hh + 64 * cc, 64)
                kt[s, pl.ds(at, 64), lanes] = value[128 + 64 * s : 192 + 64 * s]
            return carry

        lax.fori_loop(0, 4, columns, 0)
        return carry

    lax.fori_loop(0, 4, kernel_rows, 0)


def multiply(spots, weight, other_weight, kp, kt, tt_out, panel_out, corner_out, send_corner, send_panel):
    e, p, x, y, z, c = spots
    native = c == p // 8
    w = jnp.where(native, weight[0:1], other_weight[0:1]) * (1.0 / NENV)
    nt = ((1,), (1,))

    def unit(k, carry):
        first = (k + 1) // 2
        row = jnp.where(first == 1, c, 0)
        col = jnp.where(first == 0, 0, jnp.where(first == 1, 1 + c, 2))
        side = jnp.where(first == 0, c, (k + 1) % 2)
        a = halves(kt[row] * w)
        b = halves(kt[col, pl.ds(pl.multiple_of(128 * side, 128), 128)])
        tt_out[k] = dot3(a, b, nt)
        return carry

    trail = halves(kt[0, pl.ds(pl.multiple_of(128 * c, 128), 128)] * w)
    lead = halves(kp[pl.ds(pl.multiple_of(256 * c + 32 * z, 32), 32)] * w)

    def panel(i, carry):
        a = halves(kp[pl.ds(pl.multiple_of(128 * i, 128), 128)])
        corner_out[i] = dot3(lead, a, nt)
        panel_out[pl.ds(4 * i, 4)] = dot3(a, trail, nt).reshape(4, 32, 128)
        return carry

    lax.fori_loop(0, 4, panel, 0)
    send_corner()
    lax.fori_loop(0, 1, unit, 0)
    send_panel()
    lax.fori_loop(1, 5, unit, 0)


def dot_hi(a, b, dims):
    return lax.dot_general(a, b, (dims, ((), ())), precision=HI, preferred_element_type=F32)


def inverse_factor(d_ref, e_ref):
    rows = lax.broadcasted_iota(jnp.int32, (8, NB), 0)
    lanes = lax.broadcasted_iota(jnp.int32, (8, NB), 1)
    groups = NB // 8
    full = lambda v: jnp.broadcast_to(v, (8, NB))
    for g in range(groups):
        e_ref[8 * g : 8 * g + 8, :] = (lanes == rows + 8 * g).astype(F32)
    for t in range(groups):
        v = d_ref[8 * t : 8 * t + 8, :]
        e = e_ref[8 * t : 8 * t + 8, :]
        c = [full(v[:, 8 * t + i : 8 * t + i + 1]) for i in range(8)]
        v_row, e_row, c_row, inv = [], [], [], []
        pivots = jnp.ones((8, NB), F32)
        for i in range(8):
            pivot = full(c[i][i : i + 1])
            pivots = jnp.where(rows == i, pivot, pivots)
            r = 1.0 / pivot
            inv.append(r)
            v_row.append(full(v[i : i + 1]))
            e_row.append(full(e[i : i + 1]))
            c_row.append([full(c[k][i : i + 1]) if k > i else None for k in range(8)])
            if i < 7:
                m = jnp.where(rows > i, c[i] * r, 0.0)
                for k in range(i + 1, 8):
                    c[k] = c[k] - m * c_row[i][k]
                v = v - m * v_row[i]
                e = e - m * e_row[i]
        e_ref[8 * t : 8 * t + 8, :] = e * lax.rsqrt(pivots)
        for g in range(t + 1, groups):
            v = d_ref[8 * g : 8 * g + 8, :]
            e = e_ref[8 * g : 8 * g + 8, :]
            c = [full(v[:, 8 * t + i : 8 * t + i + 1]) for i in range(8)]
            for i in range(8):
                m = c[i] * inv[i]
                for k in range(i + 1, 8):
                    c[k] = c[k] - m * c_row[i][k]
                v = v - m * v_row[i]
                e = e - m * e_row[i]
            d_ref[8 * g : 8 * g + 8, :] = v
            e_ref[8 * g : 8 * g + 8, :] = e


def whole(
    desc, points, weight, panel_ref, trail_ref,
    half, other_weight, line, table, feats, feats_hi, feats_lo, rows_hi, rows_lo, kp, kt, tt, pp, cc,
    c_in, c_z, c_all, p_in, p_rows, p_cols, t_own, tt_in, tt_own, block, a, ui, uj, d, inv_ref, strip,
    half_s, half_r, swap_s, swap_r, local_s, zp_s, zp_r, zt_s, zt_r, slab_s, slab_r, slabx_s, slabx_r,
    ring_s, ring_r, ringx_s, ringx_r,
    c_s, c_r, cz_s, cz_r, cp_s, cp_r, cx_s, cx_r, keep_s,
    p_s, p_r, tt_s, tt_r, col_s, col_r, row_s, row_r, blk_s, blk_r,
):
    spots = placed()
    e, p, x, y, z, c = spots
    h = p // 8
    me = 4 * x + y
    sibling = device(x, y, z, 1 - c)
    in_plane = lambda q: device((x + q // 4) % 4, (y + q % 4) % 4, z, c)
    index_at = lambda q: 4 * ((x + q // 4) % 4) + (y + q % 4) % 4
    index_from = lambda q: 4 * ((x + 4 - q // 4) % 4) + (y + 4 - q % 4) % 4
    along_z = lambda q: device(x, y, (z + q) % 8, c)
    barrier = pltpu.get_barrier_semaphore()

    def is_me(to):
        return (to[0] == e) & (to[1] == p)

    def greet(who):
        @pl.when(jnp.logical_not(is_me(who)))
        def _():
            pl.semaphore_signal(barrier, inc=1, device_id=who, device_id_type=MESH)

    def send(src, dst, send_sem, recv_sem, to, also=None):
        here, there = is_me(to), jnp.logical_not(is_me(to))
        if also is not None:
            here, there = here & also, there & also

        @pl.when(here)
        def _():
            pltpu.make_async_copy(src, dst, recv_sem).start()

        @pl.when(there)
        def _():
            remote(src, dst, send_sem, recv_sem, to).start()

        def finish():
            @pl.when(there)
            def _():
                remote(src, dst, send_sem, recv_sem, to).wait_send()

        return finish

    z_row, z_col = e % 8, z
    apart = (z_col + 8 - z_row) % 8
    straight = apart <= 4
    gap = jnp.where(straight, apart, 8 - apart)
    z_first = jnp.where(straight, z_row, z_col)
    h_first = jnp.where(straight, e // 8, h)
    h_second = jnp.where(straight, h, e // 8)
    z_from = (z_first + 8 - jnp.where(gap == 3, 1, 0)) % 8
    c_from = jnp.where(gap == 0, h_second, jnp.where(gap >= 3, 1, 0))

    owners = []
    for k in range(5):
        first = (k + 1) // 2
        d_row = c if first == 1 else 0
        d_col = (0, 1 + 3 * c, 2 + 2 * c)[first]
        side = c if k == 0 else (k + 1) % 2
        p_a = 8 * (me // 8) + (z + d_row) % 8
        p_b = 8 * side + (z + d_col) % 8
        owners.append((2 * k, k, (p_a, p_b), None))
        if k > 0:
            owners.append((2 * k + 1, k, (p_b, p_a), None if first == 1 else c == 0))

    pl.semaphore_signal(barrier, inc=1, device_id=sibling, device_id_type=MESH)
    pl.semaphore_signal(barrier, inc=1, device_id=device(x, (y + 2) % 4, z, 1 - c), device_id_type=MESH)
    for q in range(1, 16):
        pl.semaphore_signal(barrier, inc=1, device_id=in_plane(q), device_id_type=MESH)
    for q in range(1, 8):
        pl.semaphore_signal(barrier, inc=1, device_id=along_z(q), device_id_type=MESH)
    for q in range(16):
        greet(device(q // 4, q % 4, z, h))
        greet((q, p))
        greet((q, e))
    for t in range(8):
        q = 8 * h_first + t
        greet(device(q // 4, q % 4, z_from, c_from))
    targets = [(q, 8 * c + z) for q in range(16)] + [(p, q) for q in range(16)] + [(q, p) for q in range(16)]
    expected = 24
    for to in targets:
        expected = expected + jnp.where(is_me(to), 0, 1)
    for _, _, to, also in owners:
        counts = jnp.logical_not(is_me(to)) if also is None else jnp.logical_not(is_me(to)) & also
        expected = expected + jnp.where(counts, 1, 0)
    pl.semaphore_wait(barrier, expected)

    drain = gather(
        spots, desc, points, weight, half, other_weight, line, table, feats,
        half_s, half_r, swap_s, swap_r, local_s, zp_s, zp_r, zt_s, zt_r, slab_s, slab_r, slabx_s, slabx_r,
        ring_s, ring_r, ringx_s, ringx_r,
    )
    kernel_values(spots, table, feats, feats_hi, feats_lo, rows_hi, rows_lo, kp, kt)
    pending, plain = [], []

    def go(copy):
        copy.start()
        plain.append(copy)

    def corner_rows(q):
        return pl.ds(pl.multiple_of(8 * (q // 4), 8), 8)

    def send_corner():
        stay = pltpu.make_async_copy(cc.at[me % 4, corner_rows(me)], c_in.at[me], c_r.at[0])
        stay.start()
        for q in range(1, 16):
            there = index_at(q)
            go(remote(cc.at[there % 4, corner_rows(there)], c_in.at[me], c_s.at[q], c_r.at[q], in_plane(q)))

    def send_panel():
        for q in range(16):
            pending.append(send(pp.at[q], p_in.at[me], p_s.at[q], p_r.at[me], (q, 8 * c + z)))

    multiply(spots, weight, other_weight, kp, kt, tt, pp, cc, send_corner, send_panel)

    for q in range(16):
        arrived(c_in.at[index_from(q)], c_r.at[q])
    total = c_in[0]
    for q in range(1, 16):
        total = total + c_in[q]
    at_row = 256 * c + 32 * z + 8 * (me // 4) + lax.broadcasted_iota(jnp.int32, (8, 128), 0)
    at_col = 128 * (me % 4) + lax.broadcasted_iota(jnp.int32, (8, 128), 1)
    c_z[z] = total + jnp.where(at_row == at_col, 1.0, 0.0)
    for q in range(1, 8):
        go(remote(c_z.at[z], c_z.at[z], cz_s.at[q], cz_r.at[q], along_z(q)))
    for q in range(1, 8):
        arrived(c_z.at[(z + 8 - q) % 8], cz_r.at[q])

    def corner_part(q, core):
        return c_all.at[core, :, q // 4, :, pl.ds(pl.multiple_of(128 * (q % 4), 128), 128)]

    for q in range(1, 16):
        go(remote(c_z, corner_part(me, c), cp_s.at[q], cp_r.at[q], in_plane(q)))
    go(remote(c_z, corner_part(me, c), cx_s.at[0], cx_r.at[0], sibling))
    keep = pltpu.make_async_copy(c_z, corner_part(me, c), keep_s)
    keep.start()

    for q in range(16):
        arrived(p_in.at[q], p_r.at[q])
    total = p_in[0]
    for q in range(1, 16):
        total = total + p_in[q]
    t_own[...] = total
    for q in range(16):
        pending.append(send(t_own, p_rows.at[e], row_s.at[q], row_r.at[e], (p, q)))
        pending.append(send(t_own, p_cols.at[e], col_s.at[q], col_r.at[e], (q, p)))

    for q in range(1, 16):
        part = corner_part(index_from(q), c)
        arrived(part, cp_r.at[q])
        go(remote(part, part, cx_s.at[q], cx_r.at[q], sibling))
    for q in range(16):
        go_to = device(q // 4, q % 4, z, c)
        pending.append(send(tt.at[:, 16 * q : 16 * q + 16], tt_in.at[me], tt_s.at[q], tt_r.at[me], go_to))
    keep.wait()
    for q in range(16):
        arrived(corner_part(index_from(q), 1 - c), cx_r.at[q])

    n = a.shape[0]
    a[...] = c_all[...].reshape(n, n)
    ui[:, 128:256] = a[:, pl.ds(pl.multiple_of(128 * (e // 4), 128), 128)]
    for k in range(n // NB):
        lo, hi = k * NB, (k + 1) * NB
        d[...] = a[lo:hi, lo:hi]
        inverse_factor(d, inv_ref)
        inv = inv_ref[...]
        if hi < n:
            a[lo:hi, hi:] = dot_hi(inv, a[lo:hi, hi:], ((1,), (0,)))
            u = a[lo:hi, hi:]
            a[hi:, hi:] -= dot_hi(u, u, ((0,), (0,)))
        if k == 0:
            for q in range(16):
                arrived(tt_in.at[q], tt_r.at[q])
            total = tt_in[0]
            for q in range(1, 16):
                total = total + tt_in[q]
            tt_own[...] = total
            part = me % 8
            rows = pl.ds(pl.multiple_of(16 * part, 16), 16)
            for m, kk, to, also in owners:
                pending.append(send(tt_own.at[kk], block.at[rows], blk_s.at[m], blk_r.at[part], to, also))
            for q in range(16):
                arrived(p_rows.at[q], row_r.at[q])
                arrived(p_cols.at[q], col_r.at[q])
            ui[:, 0:128] = p_rows[...].reshape(n, 128)
            uj[...] = p_cols[...].reshape(n, 128)
        ui[lo:hi, :] = dot_hi(inv, ui[lo:hi, :], ((1,), (0,)))
        uj[lo:hi, :] = dot_hi(inv, uj[lo:hi, :], ((1,), (0,)))
        if hi < n:
            ui[hi:, :] -= dot_hi(u, ui[lo:hi, :], ((0,), (0,)))
            uj[hi:, :] -= dot_hi(u, uj[lo:hi, :], ((0,), (0,)))
    for t in range(8):
        arrived(block.at[16 * t : 16 * t + 16], blk_r.at[t])
    gram = block[...]
    gram = jnp.where(straight, gram, jnp.transpose(gram))
    same = lax.broadcasted_iota(jnp.int32, (128, 128), 0) == lax.broadcasted_iota(jnp.int32, (128, 128), 1)
    gram = gram + jnp.where(same & (e == p), 1.0, 0.0)
    trail_ref[...] = gram - dot_hi(ui[:, 0:128], uj[...], ((0,), (0,)))
    across = jnp.transpose(ui[pl.ds(pl.multiple_of(32 * p, 32), 32), :])
    strip[...] = across[128:256]
    panel_ref[0:32, :] = strip[pl.ds(pl.multiple_of(32 * (e % 4), 32), 32), :]
    panel_ref[32:160, :] = across[0:128]
    for copy in plain:
        copy.wait_send()
    for finish in pending:
        finish()
    drain()


def fit(desc, points, weight):
    dma = pltpu.SemaphoreType.DMA
    vmem = pl.BlockSpec(memory_space=pltpu.VMEM)
    f32 = lambda *shape: pltpu.VMEM(shape, F32)
    bf16 = lambda *shape: pltpu.VMEM(shape, BF16)
    return pl.pallas_call(
        whole,
        out_shape=(jax.ShapeDtypeStruct((160, 32), F32), jax.ShapeDtypeStruct((128, 128), F32)),
        in_specs=[vmem] * 3,
        out_specs=[vmem] * 2,
        scratch_shapes=[
            f32(80, 64), f32(8, 1024), f32(384, 128), f32(2, 2, 384, 1024), f32(16, 64, 1024),
            bf16(1024, 1024), bf16(1024, 1024), bf16(320, 1024), bf16(320, 1024),
            f32(512, 1024), f32(3, 256, 1024), f32(5, 256, 128), f32(16, 32, 128), f32(4, 32, 128),
            f32(16, 8, 128), f32(8, 8, 128), f32(2, 8, 4, 8, 512), f32(16, 32, 128), f32(16, 32, 128), f32(16, 32, 128),
            f32(32, 128), f32(16, 5, 16, 128), f32(5, 16, 128), f32(128, 128),
            f32(512, 512), f32(512, 256), f32(512, 128), f32(NB, NB), f32(NB, NB), f32(128, 32),
            dma((3,)), dma((3,)), dma((2,)), dma((2,)), dma,
            dma((8,)), dma((8,)), dma((4,)), dma((4,)),
            dma((16,)), dma((16,)), dma((16,)), dma((16,)),
            dma((16,)), dma((16,)), dma((16,)), dma((16,)),
        ]
        + [dma((16,))] * 8
        + [dma]
        + [dma((16,))] * 10,
        compiler_params=pltpu.CompilerParams(collective_id=0, has_side_effects=True, vmem_limit_bytes=60 * 2**20),
    )(desc, points, weight)


def local(descriptors, env_weight, points):
    weight = jnp.broadcast_to(env_weight[None, :], (8, env_weight.shape[0]))
    return fit(descriptors, points, weight)


def solution(mesh):
    return jax.shard_map(
        local,
        mesh=mesh,
        in_specs=(P("pts", "env"), P("env"), P("pts", "env")),
        out_specs=(P("env", "pts"), P("env", "pts")),
        check_vma=False,
    )
```

```python
import functools

import jax
import jax.numpy as jnp
from jax import lax
from jax.experimental import pallas as pl
from jax.experimental.pallas import tpu as pltpu
from jax.sharding import PartitionSpec as P

MESH = pl.DeviceIdType.MESH
HI = lax.Precision.HIGHEST
F32 = jnp.float32
BF16 = jnp.bfloat16
NB = 128
NENV = 16384
OFFSETS = (0, 1, 2, 4)


def placed():
    e, p = lax.axis_index("env"), lax.axis_index("pts")
    x, y_lo, c = e // 4, (e // 2) % 2, e % 2
    y_hi, z = p // 8, p % 8
    return e, p, x, 2 * y_hi + y_lo, z, c


def device(x, y, z, c):
    return (4 * x + 2 * (y % 2) + c, 8 * (y // 2) + z)


def remote(src, dst, send_sem, recv_sem, to):
    return pltpu.make_async_remote_copy(
        src_ref=src, dst_ref=dst, send_sem=send_sem, recv_sem=recv_sem, device_id=to, device_id_type=MESH
    )


def arrived(ref, sem):
    pltpu.make_async_copy(ref, ref, sem).wait()


def halves(a):
    hi = a.astype(BF16)
    return hi, (a - hi.astype(F32)).astype(BF16)


def dot3(a, b, dims):
    one = lambda l, r: lax.dot_general(l, r, (dims, ((), ())), preferred_element_type=F32)
    return one(a[0], b[0]) + (one(a[0], b[1]) + one(a[1], b[0]))


def gather(
    spots, desc, points, weight,
    half, other_weight, line, table, extra, feats, feats_hi, feats_lo, rows_hi, rows_lo,
    half_s, half_r, swap_s, swap_r, zp_s, zp_r, zt_s, zt_r, slab_s, slab_r, slabx_s, slabx_r,
    ring_s, ring_r, ringx_s, ringx_r,
):
    e, p, x, y, z, c = spots
    h = p // 8
    native = c == h
    turn = jnp.where(native, 1, 7)
    sibling = device(x, y, z, 1 - c)
    partner = device(x, (y + 2) % 4, z, 1 - c)
    along_z = lambda d: device(x, y, (z + d) % 8, c)

    def step(j1, j2):
        return (x + j1 * (1 - c) + j2 * c) % 4, (y + j1 * c + j2 * (1 - c)) % 4

    def slab_of(j1, j2, core):
        sx = (x + 8 - j1 * (1 - core) - j2 * core) % 4
        sy = (y + 8 - j1 * core - j2 * (1 - core)) % 4
        lanes = pl.multiple_of(128 * (2 * sx + sy % 2), 128)
        return sy // 2, pl.ds(lanes, 128)

    o = 1 - c
    to_sibling = [
        remote(points.at[pl.ds(pl.multiple_of(16 * o, 16), 16)], half.at[0:16], half_s.at[0], half_r.at[0], sibling),
        remote(points.at[pl.ds(pl.multiple_of(32 + 64 * o, 32), 64)], half.at[16:80], half_s.at[1], half_r.at[1], sibling),
        remote(weight, other_weight, half_s.at[2], half_r.at[2], sibling),
    ]
    for copy in to_sibling:
        copy.start()
    parts = [pl.ds(32 * n, 32) for n in range(2)]
    swap = [remote(desc.at[r], feats.at[p, r], swap_s.at[n], swap_r.at[n], partner) for n, r in enumerate(parts)]
    keep = [pltpu.make_async_copy(desc.at[r], feats.at[p, r], swap_r.at[n]) for n, r in enumerate(parts)]

    def piece(m, n, core, sign):
        d = (0, 1, 2, 3, 4, 7, 6, 5)[m]
        return feats.at[8 * core + (z + 8 * 8 - sign * d) % 8, parts[n]]

    def first_sends(src, n):
        dst = piece(0, n, c, turn)
        return [
            remote(src, dst, ring_s.at[2 + n], ring_r.at[2 + n], along_z(turn)),
            remote(src, dst, ring_s.at[10 + n], ring_r.at[10 + n], along_z(8 - turn)),
            remote(src, dst, ringx_s.at[n], ringx_r.at[n], sibling),
        ]

    first = [first_sends(piece(0, n, c, turn), n) for n in range(2)]

    @pl.when(native)
    def _():
        for n in range(2):
            for copy in first_sends(desc.at[parts[n]], n):
                copy.start()
        for copy in keep:
            copy.start()

    @pl.when(jnp.logical_not(native))
    def _():
        for copy in swap:
            copy.start()

    arrived(half.at[0:16], half_r.at[0])
    arrived(half.at[16:80], half_r.at[1])
    mine = jnp.concatenate(
        [points[pl.ds(pl.multiple_of(16 * c, 16), 16)], points[pl.ds(pl.multiple_of(32 + 64 * c, 32), 64)]], axis=0
    )
    theirs = half[...]
    packed = jnp.where(c == 0, jnp.concatenate([mine, theirs], axis=1), jnp.concatenate([theirs, mine], axis=1))
    own_panel = line.at[pl.ds(pl.multiple_of(16 * z, 16), 16)]
    line[pl.ds(pl.multiple_of(16 * z, 16), 16)] = packed[0:16]
    line[128:192] = packed[16:80]

    lined = []
    for s in (1, 2, 3):
        rows = pl.ds(128 + 64 * s, 64)
        lined.append(remote(line.at[128:192], line.at[rows], zt_s.at[s], zt_r.at[s], along_z(8 - OFFSETS[s])))
    for d in range(1, 8):
        lined.append(remote(own_panel, own_panel, zp_s.at[d], zp_r.at[d], along_z(d)))
    for copy in lined:
        copy.start()

    rings, across = [], []

    def pass_on(m, n):
        src = piece(m, n, c, turn)
        if m in (1, 2, 3):
            at = 2 * (m + 1) + n
            rings.append(remote(src, src, ring_s.at[at], ring_r.at[at], along_z(turn)))
            rings[-1].start()
        if m in (5, 6):
            at = 2 * (m + 1) + n
            rings.append(remote(src, src, ring_s.at[at], ring_r.at[at], along_z(8 - turn)))
            rings[-1].start()
        at = 2 * m + n
        across.append(remote(src, src, ringx_s.at[at], ringx_r.at[at], sibling))
        across[-1].start()

    @pl.when(jnp.logical_not(native))
    def _():
        for n in range(2):
            arrived(piece(0, n, c, turn), swap_r.at[n])
            for copy in first[n]:
                copy.start()

    for s in (1, 2, 3):
        arrived(line.at[pl.ds(128 + 64 * s, 64)], zt_r.at[s])
    for d in range(1, 8):
        rows = pl.ds(pl.multiple_of(16 * ((z + 8 - d) % 8), 16), 16)
        arrived(line.at[rows], zp_r.at[d])

    slabs = []

    def forward(src, dst, j1, j2, to):
        n = 4 * j1 + j2
        slabs.append(remote(src, dst, slab_s.at[n], slab_r.at[n], device(*to, z, c)))
        slabs[-1].start()

    def third(core):
        return pl.ds(pl.multiple_of(256 + 64 * core, 64), 64)

    def to_other_core(n, src, at):
        slabs.append(remote(src, extra.at[at[0], :, at[1]], slabx_s.at[n], slabx_r.at[n], sibling))
        slabs[-1].start()

    def split(value, rows, lanes):
        hi, lo = halves(value)
        rows_hi[rows, lanes] = hi
        rows_lo[rows, lanes] = lo

    def split_third(value, hh, cc, lanes):
        split(value, pl.ds(pl.multiple_of(512 + 128 * hh + 64 * cc, 64), 64), lanes)

    def split_piece(m, core, sign):
        d = (0, 1, 2, 3, 4, 7, 6, 5)[m]
        slot = 8 * core + (z + 8 * 8 - sign * d) % 8
        hi, lo = halves(feats[slot])
        at = pl.ds(pl.multiple_of(64 * slot, 64), 64)
        feats_hi[at] = hi
        feats_lo[at] = lo

    mine_h, mine_lanes = slab_of(0, 0, c)
    own = table.at[mine_h, :, mine_lanes]
    forward(line, own, 1, 0, step(1, 0))
    forward(line, own, 3, 0, step(3, 0))
    forward(line, own, 0, 1, step(0, 1))
    forward(line, own, 0, 3, step(0, 3))
    to_other_core(0, line.at[third(o)], (mine_h, mine_lanes))
    split(line[0:256], pl.ds(pl.multiple_of(256 * mine_h, 256), 256), mine_lanes)
    split_third(line[third(c)], mine_h, c, mine_lanes)

    def take_piece(m):
        for n in range(2):
            arrived(piece(m, n, c, turn), ring_r.at[2 * m + n])
            pass_on(m, n)
        split_piece(m, c, turn)

    def take_slab(j1, j2):
        hh, lanes = slab_of(j1, j2, c)
        here = table.at[hh, :, lanes]
        arrived(here, slab_r.at[4 * j1 + j2])
        if j2 == 0:
            if j1 == 1:
                forward(here, here, 2, 0, step(1, 0))
            forward(here, here, j1, 1, step(0, 1))
            forward(here, here, j1, 3, step(0, 3))
        if j2 == 1 and j1 in (0, 1):
            forward(here, here, j1, 2, step(0, 1))
        if j2 == 3 and j1 in (2, 3):
            forward(here, here, j1, 2, step(0, 3))
        to_other_core(4 * j1 + j2, table.at[hh, third(o), lanes], (hh, lanes))
        split(table[hh, 0:256, lanes], pl.ds(pl.multiple_of(256 * hh, 256), 256), lanes)
        split_third(table[hh, third(c), lanes], hh, c, lanes)

    take_slab(1, 0)
    take_slab(3, 0)
    take_piece(1)
    take_piece(5)
    take_slab(0, 1)
    take_slab(0, 3)
    take_slab(2, 0)
    take_slab(1, 1)
    take_slab(3, 3)
    take_piece(2)
    take_piece(6)
    take_slab(1, 3)
    take_slab(3, 1)
    take_slab(2, 3)
    take_slab(2, 1)
    take_slab(0, 2)
    take_piece(3)
    take_piece(7)
    take_slab(1, 2)
    take_slab(3, 2)
    take_slab(2, 2)
    take_piece(4)

    @pl.when(native)
    def _():
        for n in range(2):
            arrived(piece(0, n, c, turn), swap_r.at[n])

    split_piece(0, c, turn)
    for m in (0, 1, 5, 2, 6, 3, 7, 4):
        for n in range(2):
            arrived(piece(m, n, o, 8 - turn), ringx_r.at[2 * m + n])
        split_piece(m, o, 8 - turn)
    for j1 in range(4):
        for j2 in range(4):
            hh, lanes = slab_of(j1, j2, o)
            arrived(extra.at[hh, :, lanes], slabx_r.at[4 * j1 + j2])
            split_third(extra[hh, :, lanes], hh, o, lanes)
    arrived(other_weight, half_r.at[2])

    def drain():
        for copy in to_sibling + lined + rings + across + slabs + first[0] + first[1]:
            copy.wait_send()

        @pl.when(jnp.logical_not(native))
        def _():
            for copy in swap:
                copy.wait_send()

    return drain


def kernel_values(spots, feats_hi, feats_lo, rows_hi, rows_lo, kp, kt, kp_s, kp_r, kt_s, kt_r):
    e, p, x, y, z, c = spots
    sibling = device(x, y, z, 1 - c)

    def values(rows, lanes):
        scaled = dot3((rows_hi[rows], rows_lo[rows]), (feats_hi[:, lanes], feats_lo[:, lanes]), ((1,), (0,))) * (1.0 / 32.0)
        return 0.25 * scaled * scaled * scaled

    sent = []

    def exchange(t):
        lanes = pl.ds(256 * t, 256)
        lead, trail = kp.at[:, :, c, :, lanes], kt.at[0:2, :, c, :, lanes]
        sent.append(remote(lead, lead, kp_s.at[t], kp_r.at[t], sibling))
        sent.append(remote(trail, trail, kt_s.at[t], kt_r.at[t], sibling))
        sent[-2].start()
        sent[-1].start()

    for t in range(4):
        lanes = pl.ds(256 * t, 256)
        value = values(pl.ds(0, 512), lanes)
        for hh in range(2):
            kp[hh, :, c, :, lanes] = value[256 * hh : 256 * hh + 128].reshape(8, 16, 256)
            kt[0:2, hh, c, :, lanes] = value[256 * hh + 128 : 256 * hh + 256].reshape(2, 64, 256)
        if t > 0:
            exchange(t - 1)
    for t in range(2):
        lanes = pl.ds(512 * t, 512)
        value = values(pl.ds(512, 256), lanes)
        kt[2, :, :, :, lanes] = value.reshape(2, 2, 64, 512)
        if t == 0:
            exchange(3)
    for t in range(4):
        lanes = pl.ds(256 * t, 256)
        arrived(kp.at[:, :, 1 - c, :, lanes], kp_r.at[t])
        arrived(kt.at[0:2, :, 1 - c, :, lanes], kt_r.at[t])

    def drain():
        for copy in sent:
            copy.wait_send()

    return drain


def multiply(spots, weight, other_weight, kp, kt, tt_out, panel_out, corner_out, send_corner):
    e, p, x, y, z, c = spots
    native = c == p // 8
    w = jnp.where(native, weight[0:1], other_weight[0:1]) * (1.0 / NENV)
    nt = ((1,), (1,))

    def unit(k, carry):
        first = (k + 1) // 2
        row = jnp.where(first == 1, c, 0)
        col = jnp.where(first == 0, 0, jnp.where(first == 1, 1 + c, 2))
        side = jnp.where(first == 0, c, (k + 1) % 2)
        a = halves(kt[row].reshape(256, 1024) * w)
        b = halves(kt[col, side].reshape(128, 1024))
        tt_out[k] = dot3(a, b, nt)
        return carry

    trail = halves(kt[0, c].reshape(128, 1024) * w)
    lead = halves(kp[c, z].reshape(32, 1024) * w)

    def panel(i, carry):
        a = halves(kp[i // 2, pl.ds(4 * (i % 2), 4)].reshape(128, 1024))
        corner_out[i] = dot3(lead, a, nt)
        panel_out[pl.ds(4 * i, 4)] = dot3(a, trail, nt).reshape(4, 32, 128)
        return carry

    lax.fori_loop(0, 4, panel, 0)
    send_corner()
    lax.fori_loop(0, 5, unit, 0)


def dot_hi(a, b, dims):
    return lax.dot_general(a, b, (dims, ((), ())), precision=HI, preferred_element_type=F32)


def inverse_factor(d_ref, e_ref):
    rows = lax.broadcasted_iota(jnp.int32, (8, NB), 0)
    lanes = lax.broadcasted_iota(jnp.int32, (8, NB), 1)
    groups = NB // 8
    full = lambda v: jnp.broadcast_to(v, (8, NB))
    for g in range(groups):
        e_ref[8 * g : 8 * g + 8, :] = (lanes == rows + 8 * g).astype(F32)
    for t in range(groups):
        v = d_ref[8 * t : 8 * t + 8, :]
        e = e_ref[8 * t : 8 * t + 8, :]
        c = [full(v[:, 8 * t + i : 8 * t + i + 1]) for i in range(8)]
        v_row, e_row, c_row, inv = [], [], [], []
        pivots = jnp.ones((8, NB), F32)
        for i in range(8):
            pivot = full(c[i][i : i + 1])
            pivots = jnp.where(rows == i, pivot, pivots)
            r = 1.0 / pivot
            inv.append(r)
            v_row.append(full(v[i : i + 1]))
            e_row.append(full(e[i : i + 1]))
            c_row.append([full(c[k][i : i + 1]) if k > i else None for k in range(8)])
            if i < 7:
                m = jnp.where(rows > i, c[i] * r, 0.0)
                for k in range(i + 1, 8):
                    c[k] = c[k] - m * c_row[i][k]
                v = v - m * v_row[i]
                e = e - m * e_row[i]
        e_ref[8 * t : 8 * t + 8, :] = e * lax.rsqrt(pivots)
        for g in range(t + 1, groups):
            v = d_ref[8 * g : 8 * g + 8, :]
            e = e_ref[8 * g : 8 * g + 8, :]
            c = [full(v[:, 8 * t + i : 8 * t + i + 1]) for i in range(8)]
            for i in range(8):
                m = c[i] * inv[i]
                for k in range(i + 1, 8):
                    c[k] = c[k] - m * c_row[i][k]
                v = v - m * v_row[i]
                e = e - m * e_row[i]
            d_ref[8 * g : 8 * g + 8, :] = v
            e_ref[8 * g : 8 * g + 8, :] = e


def whole(
    desc, points_t, weight, panel_ref, trail_ref,
    points, half, other_weight, line, table, extra, feats, feats_hi, feats_lo, rows_hi, rows_lo, kp, kt, tt, pp, cc,
    c_in, c_z, c_all, p_in, p_rows, p_cols, t_own, tt_in, tt_own, block, a, ui, uj, d, inv_ref,
    half_s, half_r, swap_s, swap_r, zp_s, zp_r, zt_s, zt_r, slab_s, slab_r, slabx_s, slabx_r,
    ring_s, ring_r, ringx_s, ringx_r, kp_s, kp_r, kt_s, kt_r,
    c_s, c_r, cz_s, cz_r, cp_s, cp_r, cx_s, cx_r, keep_s,
    p_s, p_r, tt_s, tt_r, col_s, col_r, row_s, row_r, blk_s, blk_r,
):
    spots = placed()
    e, p, x, y, z, c = spots
    h = p // 8
    me = 4 * x + y
    sibling = device(x, y, z, 1 - c)
    in_plane = lambda q: device((x + q // 4) % 4, (y + q % 4) % 4, z, c)
    index_at = lambda q: 4 * ((x + q // 4) % 4) + (y + q % 4) % 4
    index_from = lambda q: 4 * ((x + 4 - q // 4) % 4) + (y + 4 - q % 4) % 4
    along_z = lambda q: device(x, y, (z + q) % 8, c)
    barrier = pltpu.get_barrier_semaphore()

    def is_me(to):
        return (to[0] == e) & (to[1] == p)

    def send(src, dst, send_sem, recv_sem, to, also=None):
        here, there = is_me(to), jnp.logical_not(is_me(to))
        if also is not None:
            here, there = here & also, there & also

        @pl.when(here)
        def _():
            pltpu.make_async_copy(src, dst, recv_sem).start()

        @pl.when(there)
        def _():
            remote(src, dst, send_sem, recv_sem, to).start()

        def finish():
            @pl.when(there)
            def _():
                remote(src, dst, send_sem, recv_sem, to).wait_send()

        return finish

    z_row, z_col = e % 8, z
    apart = (z_col + 8 - z_row) % 8
    straight = apart <= 4
    owners = []
    for k in range(5):
        first = (k + 1) // 2
        d_row = c if first == 1 else 0
        d_col = (0, 1 + 3 * c, 2 + 2 * c)[first]
        side = c if k == 0 else (k + 1) % 2
        p_a = 8 * (me // 8) + (z + d_row) % 8
        p_b = 8 * side + (z + d_col) % 8
        owners.append((2 * k, k, (p_a, p_b), None))
        if k > 0:
            owners.append((2 * k + 1, k, (p_b, p_a), None if first == 1 else c == 0))

    pl.semaphore_signal(barrier, inc=1, device_id=sibling, device_id_type=MESH)
    pl.semaphore_signal(barrier, inc=1, device_id=device(x, (y + 2) % 4, z, 1 - c), device_id_type=MESH)
    for q in range(1, 16):
        pl.semaphore_signal(barrier, inc=1, device_id=in_plane(q), device_id_type=MESH)
    for q in range(1, 8):
        pl.semaphore_signal(barrier, inc=1, device_id=along_z(q), device_id_type=MESH)
    points[...] = jnp.transpose(points_t[...])
    pl.semaphore_wait(barrier, 24)

    drain = gather(
        spots, desc, points, weight, half, other_weight, line, table, extra, feats, feats_hi, feats_lo, rows_hi, rows_lo,
        half_s, half_r, swap_s, swap_r, zp_s, zp_r, zt_s, zt_r, slab_s, slab_r, slabx_s, slabx_r,
        ring_s, ring_r, ringx_s, ringx_r,
    )
    drain_values = kernel_values(spots, feats_hi, feats_lo, rows_hi, rows_lo, kp, kt, kp_s, kp_r, kt_s, kt_r)
    pending, plain = [], []

    def go(copy):
        copy.start()
        plain.append(copy)

    def corner_rows(q):
        return pl.ds(pl.multiple_of(8 * (q // 4), 8), 8)

    def send_corner():
        stay = pltpu.make_async_copy(cc.at[me % 4, corner_rows(me)], c_in.at[me], c_r.at[0])
        stay.start()
        for q in range(1, 16):
            there = index_at(q)
            go(remote(cc.at[there % 4, corner_rows(there)], c_in.at[me], c_s.at[q], c_r.at[q], in_plane(q)))

    multiply(spots, weight, other_weight, kp, kt, tt, pp, cc, send_corner)

    for q in range(16):
        arrived(c_in.at[index_from(q)], c_r.at[q])
    total = c_in[0]
    for q in range(1, 16):
        total = total + c_in[q]
    at_row = 256 * c + 32 * z + 8 * (me // 4) + lax.broadcasted_iota(jnp.int32, (8, 128), 0)
    at_col = 128 * (me % 4) + lax.broadcasted_iota(jnp.int32, (8, 128), 1)
    c_z[z] = total + jnp.where(at_row == at_col, 1.0, 0.0)
    for q in range(1, 8):
        go(remote(c_z.at[z], c_z.at[z], cz_s.at[q], cz_r.at[q], along_z(q)))
    pending.append(send(pp.at[e], p_in.at[me], p_s.at[0], p_r.at[me], (e, 8 * c + z)))
    for q in range(1, 16):
        go(remote(pp.at[(e + q) % 16], p_in.at[me], p_s.at[q], p_r.at[me], ((e + q) % 16, 8 * c + z)))
    for q in range(1, 8):
        arrived(c_z.at[(z + 8 - q) % 8], cz_r.at[q])

    def corner_part(q, core):
        return c_all.at[core, :, q // 4, :, pl.ds(pl.multiple_of(128 * (q % 4), 128), 128)]

    for q in range(1, 16):
        go(remote(c_z, corner_part(me, c), cp_s.at[q], cp_r.at[q], in_plane(q)))
    go(remote(c_z, corner_part(me, c), cx_s.at[0], cx_r.at[0], sibling))
    keep = pltpu.make_async_copy(c_z, corner_part(me, c), keep_s)
    keep.start()

    for q in range(1, 16):
        part = corner_part(index_from(q), c)
        arrived(part, cp_r.at[q])
        go(remote(part, part, cx_s.at[q], cx_r.at[q], sibling))
    for q in range(16):
        arrived(p_in.at[q], p_r.at[q])
    total = p_in[0]
    for q in range(1, 16):
        total = total + p_in[q]
    t_own[...] = total
    pending.append(send(t_own, p_rows.at[e], row_s.at[0], row_r.at[e], (p, p)))
    pending.append(send(t_own, p_cols.at[e], col_s.at[0], col_r.at[e], (e, p)))
    for q in range(1, 16):
        go(remote(t_own, p_rows.at[e], row_s.at[q], row_r.at[e], (p, (p + q) % 16)))
        go(remote(t_own, p_cols.at[e], col_s.at[q], col_r.at[e], ((e + q) % 16, p)))
    stay_tt = pltpu.make_async_copy(tt.at[:, pl.ds(pl.multiple_of(16 * me, 16), 16)], tt_in.at[me], tt_r.at[me])
    stay_tt.start()
    for q in range(1, 16):
        rows = pl.ds(pl.multiple_of(16 * index_at(q), 16), 16)
        go(remote(tt.at[:, rows], tt_in.at[me], tt_s.at[q], tt_r.at[me], in_plane(q)))
    keep.wait()
    for q in range(16):
        arrived(corner_part(index_from(q), 1 - c), cx_r.at[q])

    n = a.shape[0]
    a[...] = c_all[...].reshape(n, n)
    ui[:, 128:256] = a[:, pl.ds(pl.multiple_of(128 * (e // 4), 128), 128)]
    def apply(k):
        lo, hi = k * NB, (k + 1) * NB
        inv = inv_ref[k]
        ui[lo:hi, :] = dot_hi(inv, ui[lo:hi, :], ((1,), (0,)))
        uj[lo:hi, :] = dot_hi(inv, uj[lo:hi, :], ((1,), (0,)))
        if hi < n:
            u = a[lo:hi, hi:]
            ui[hi:, :] -= dot_hi(u, ui[lo:hi, :], ((0,), (0,)))
            uj[hi:, :] -= dot_hi(u, uj[lo:hi, :], ((0,), (0,)))

    for k in range(n // NB):
        lo, hi = k * NB, (k + 1) * NB
        d[...] = a[lo:hi, lo:hi]
        inverse_factor(d, inv_ref.at[k])
        if k >= 2:
            apply(k - 1)
        if hi < n:
            a[lo:hi, hi:] = dot_hi(inv_ref[k], a[lo:hi, hi:], ((1,), (0,)))
            u = a[lo:hi, hi:]
            a[hi:, hi:] -= dot_hi(u, u, ((0,), (0,)))
        if k == 1:
            for q in range(16):
                arrived(tt_in.at[q], tt_r.at[q])
            total = tt_in[0]
            for q in range(1, 16):
                total = total + tt_in[q]
            tt_own[...] = total
            part = me % 8
            rows = pl.ds(pl.multiple_of(16 * part, 16), 16)
            for m, kk, to, also in owners:
                pending.append(send(tt_own.at[kk], block.at[rows], blk_s.at[m], blk_r.at[part], to, also))
            for q in range(16):
                arrived(p_rows.at[q], row_r.at[q])
                arrived(p_cols.at[q], col_r.at[q])
            ui[:, 0:128] = p_rows[...].reshape(n, 128)
            uj[...] = p_cols[...].reshape(n, 128)
            apply(0)
    apply(n // NB - 1)
    for t in range(8):
        arrived(block.at[16 * t : 16 * t + 16], blk_r.at[t])
    gram = block[...]
    gram = jnp.where(straight, gram, jnp.transpose(gram))
    same = lax.broadcasted_iota(jnp.int32, (128, 128), 0) == lax.broadcasted_iota(jnp.int32, (128, 128), 1)
    gram = gram + jnp.where(same & (e == p), 1.0, 0.0)
    trail_ref[...] = gram - dot_hi(ui[:, 0:128], uj[...], ((0,), (0,)))
    own_rows = ui[pl.ds(pl.multiple_of(32 * p, 32), 32), :]
    lead = pltpu.roll(own_rows[:, 128:256], (128 - 32 * (e % 4)) % 128, 1)
    rest = pltpu.roll(own_rows[:, 0:128], 32, 1)
    lanes = lax.broadcasted_iota(jnp.int32, (32, 128), 1)
    panel_ref[:, 0:128] = jnp.where(lanes < 32, lead, rest)
    panel_ref[:, 128:160] = rest[:, 0:32]
    for copy in plain:
        copy.wait_send()
    for finish in pending:
        finish()
    drain()
    drain_values()


def fit(desc, points_t, weight):
    dma = pltpu.SemaphoreType.DMA
    vmem = pl.BlockSpec(memory_space=pltpu.VMEM)
    f32 = lambda *shape: pltpu.VMEM(shape, F32)
    bf16 = lambda *shape: pltpu.VMEM(shape, BF16)
    return pl.pallas_call(
        whole,
        out_shape=(jax.ShapeDtypeStruct((32, 160), F32), jax.ShapeDtypeStruct((128, 128), F32)),
        in_specs=[vmem] * 3,
        out_specs=[vmem] * 2,
        scratch_shapes=[
            f32(160, 64), f32(80, 64), f32(1, 1024), f32(384, 128), f32(2, 384, 1024), f32(2, 64, 1024), f32(16, 64, 1024),
            bf16(1024, 1024), bf16(1024, 1024), bf16(768, 1024), bf16(768, 1024),
            f32(2, 8, 2, 16, 1024), f32(3, 2, 2, 64, 1024), f32(5, 256, 128), f32(16, 32, 128), f32(4, 32, 128),
            f32(16, 8, 128), f32(8, 8, 128), f32(2, 8, 4, 8, 512), f32(16, 32, 128), f32(16, 32, 128), f32(16, 32, 128),
            f32(32, 128), f32(16, 5, 16, 128), f32(5, 16, 128), f32(128, 128),
            f32(512, 512), f32(512, 256), f32(512, 128), f32(NB, NB), f32(4, NB, NB),
            dma((3,)), dma((3,)), dma((2,)), dma((2,)),
            dma((8,)), dma((8,)), dma((4,)), dma((4,)),
            dma((16,)), dma((16,)), dma((16,)), dma((16,)),
            dma((16,)), dma((16,)), dma((16,)), dma((16,)),
            dma((4,)), dma((4,)), dma((4,)), dma((4,)),
        ]
        + [dma((16,))] * 8
        + [dma]
        + [dma((16,))] * 10,
        compiler_params=pltpu.CompilerParams(collective_id=0, has_side_effects=True, vmem_limit_bytes=60 * 2**20),
    )(desc, points_t, weight)


def local(descriptors, env_weight, points):
    panel_t, trailing = fit(descriptors, points.T, env_weight.reshape(1, -1))
    return panel_t.T, trailing


def solution(mesh):
    return jax.shard_map(
        local,
        mesh=mesh,
        in_specs=(P("pts", "env"), P("env"), P("pts", "env")),
        out_specs=(P("env", "pts"), P("env", "pts")),
        check_vma=False,
    )
```

```python
import functools

import jax
import jax.numpy as jnp
from jax import lax
from jax.experimental import pallas as pl
from jax.experimental.pallas import tpu as pltpu
from jax.sharding import PartitionSpec as P

MESH = pl.DeviceIdType.MESH
HI = lax.Precision.HIGHEST
F32 = jnp.float32
BF16 = jnp.bfloat16
NB = 128
NENV = 16384
OFFSETS = (0, 1, 2, 4)


def placed():
    e, p = lax.axis_index("env"), lax.axis_index("pts")
    x, y_lo, c = e // 4, (e // 2) % 2, e % 2
    y_hi, z = p // 8, p % 8
    return e, p, x, 2 * y_hi + y_lo, z, c


def device(x, y, z, c):
    return (4 * x + 2 * (y % 2) + c, 8 * (y // 2) + z)


def remote(src, dst, send_sem, recv_sem, to):
    return pltpu.make_async_remote_copy(
        src_ref=src, dst_ref=dst, send_sem=send_sem, recv_sem=recv_sem, device_id=to, device_id_type=MESH
    )


def arrived(ref, sem):
    pltpu.make_async_copy(ref, ref, sem).wait()


def halves(a):
    hi = a.astype(BF16)
    return hi, (a - hi.astype(F32)).astype(BF16)


def dot3(a, b, dims):
    one = lambda l, r: lax.dot_general(l, r, (dims, ((), ())), preferred_element_type=F32)
    return one(a[0], b[0]) + (one(a[0], b[1]) + one(a[1], b[0]))


def gather(
    spots, desc, points, weight,
    half, other_weight, line, table, extra, feats, feats_hi, feats_lo, rows_hi, rows_lo,
    half_s, half_r, swap_s, swap_r, zp_s, zp_r, zt_s, zt_r, slab_s, slab_r, slabx_s, slabx_r,
    ring_s, ring_r, ringx_s, ringx_r,
):
    e, p, x, y, z, c = spots
    h = p // 8
    native = c == h
    turn = jnp.where(native, 1, 7)
    sibling = device(x, y, z, 1 - c)
    partner = device(x, (y + 2) % 4, z, 1 - c)
    along_z = lambda d: device(x, y, (z + d) % 8, c)

    def step(j1, j2):
        return (x + j1 * (1 - c) + j2 * c) % 4, (y + j1 * c + j2 * (1 - c)) % 4

    def slab_of(j1, j2, core):
        sx = (x + 8 - j1 * (1 - core) - j2 * core) % 4
        sy = (y + 8 - j1 * core - j2 * (1 - core)) % 4
        lanes = pl.multiple_of(128 * (2 * sx + sy % 2), 128)
        return sy // 2, pl.ds(lanes, 128)

    o = 1 - c
    to_sibling = [
        remote(points.at[pl.ds(pl.multiple_of(16 * o, 16), 16)], half.at[0:16], half_s.at[0], half_r.at[0], sibling),
        remote(points.at[pl.ds(pl.multiple_of(32 + 64 * o, 32), 64)], half.at[16:80], half_s.at[1], half_r.at[1], sibling),
        remote(weight, other_weight, half_s.at[2], half_r.at[2], sibling),
    ]
    for copy in to_sibling:
        copy.start()
    parts = [pl.ds(32 * n, 32) for n in range(2)]
    swap = [remote(desc.at[r], feats.at[p, r], swap_s.at[n], swap_r.at[n], partner) for n, r in enumerate(parts)]
    keep = [pltpu.make_async_copy(desc.at[r], feats.at[p, r], swap_r.at[n]) for n, r in enumerate(parts)]

    def piece(m, n, core, sign):
        d = (0, 1, 2, 3, 4, 7, 6, 5)[m]
        return feats.at[8 * core + (z + 8 * 8 - sign * d) % 8, parts[n]]

    def first_sends(src, n):
        dst = piece(0, n, c, turn)
        return [
            remote(src, dst, ring_s.at[2 + n], ring_r.at[2 + n], along_z(turn)),
            remote(src, dst, ring_s.at[10 + n], ring_r.at[10 + n], along_z(8 - turn)),
            remote(src, dst, ringx_s.at[n], ringx_r.at[n], sibling),
        ]

    first = [first_sends(piece(0, n, c, turn), n) for n in range(2)]

    @pl.when(native)
    def _():
        for n in range(2):
            for copy in first_sends(desc.at[parts[n]], n):
                copy.start()
        for copy in keep:
            copy.start()

    @pl.when(jnp.logical_not(native))
    def _():
        for copy in swap:
            copy.start()

    arrived(half.at[0:16], half_r.at[0])
    arrived(half.at[16:80], half_r.at[1])
    mine = jnp.concatenate(
        [points[pl.ds(pl.multiple_of(16 * c, 16), 16)], points[pl.ds(pl.multiple_of(32 + 64 * c, 32), 64)]], axis=0
    )
    theirs = half[...]
    packed = jnp.where(c == 0, jnp.concatenate([mine, theirs], axis=1), jnp.concatenate([theirs, mine], axis=1))
    own_panel = line.at[pl.ds(pl.multiple_of(16 * z, 16), 16)]
    line[pl.ds(pl.multiple_of(16 * z, 16), 16)] = packed[0:16]
    line[128:192] = packed[16:80]

    lined = []
    for s in (1, 2, 3):
        rows = pl.ds(128 + 64 * s, 64)
        lined.append(remote(line.at[128:192], line.at[rows], zt_s.at[s], zt_r.at[s], along_z(8 - OFFSETS[s])))
    for d in range(1, 8):
        lined.append(remote(own_panel, own_panel, zp_s.at[d], zp_r.at[d], along_z(d)))
    for copy in lined:
        copy.start()

    rings, across = [], []

    def pass_on(m, n):
        src = piece(m, n, c, turn)
        if m in (1, 2, 3):
            at = 2 * (m + 1) + n
            rings.append(remote(src, src, ring_s.at[at], ring_r.at[at], along_z(turn)))
            rings[-1].start()
        if m in (5, 6):
            at = 2 * (m + 1) + n
            rings.append(remote(src, src, ring_s.at[at], ring_r.at[at], along_z(8 - turn)))
            rings[-1].start()
        at = 2 * m + n
        across.append(remote(src, src, ringx_s.at[at], ringx_r.at[at], sibling))
        across[-1].start()

    for s in (1, 2, 3):
        arrived(line.at[pl.ds(128 + 64 * s, 64)], zt_r.at[s])
    for d in range(1, 8):
        rows = pl.ds(pl.multiple_of(16 * ((z + 8 - d) % 8), 16), 16)
        arrived(line.at[rows], zp_r.at[d])

    slabs = []

    def forward(src, dst, j1, j2, to):
        n = 4 * j1 + j2
        slabs.append(remote(src, dst, slab_s.at[n], slab_r.at[n], device(*to, z, c)))
        slabs[-1].start()

    def third(core):
        return pl.ds(pl.multiple_of(256 + 64 * core, 64), 64)

    def to_other_core(n, src, at):
        slabs.append(remote(src, extra.at[at[0], :, at[1]], slabx_s.at[n], slabx_r.at[n], sibling))
        slabs[-1].start()

    def split(value, rows, lanes):
        hi, lo = halves(value)
        rows_hi[rows, lanes] = hi
        rows_lo[rows, lanes] = lo

    def split_third(value, hh, cc, lanes):
        split(value, pl.ds(pl.multiple_of(512 + 128 * hh + 64 * cc, 64), 64), lanes)

    def split_piece(m, core, sign):
        d = (0, 1, 2, 3, 4, 7, 6, 5)[m]
        slot = 8 * core + (z + 8 * 8 - sign * d) % 8
        hi, lo = halves(feats[slot])
        at = pl.ds(pl.multiple_of(64 * slot, 64), 64)
        feats_hi[at] = hi
        feats_lo[at] = lo

    mine_h, mine_lanes = slab_of(0, 0, c)
    own = table.at[mine_h, :, mine_lanes]
    forward(line, own, 1, 0, step(1, 0))
    forward(line, own, 3, 0, step(3, 0))
    forward(line, own, 0, 1, step(0, 1))
    forward(line, own, 0, 3, step(0, 3))
    to_other_core(0, line.at[third(o)], (mine_h, mine_lanes))
    @pl.when(jnp.logical_not(native))
    def _():
        for n in range(2):
            arrived(piece(0, n, c, turn), swap_r.at[n])
            for copy in first[n]:
                copy.start()

    split(line[0:256], pl.ds(pl.multiple_of(256 * mine_h, 256), 256), mine_lanes)
    split_third(line[third(c)], mine_h, c, mine_lanes)

    def take_piece(m):
        for n in range(2):
            arrived(piece(m, n, c, turn), ring_r.at[2 * m + n])
            pass_on(m, n)
        split_piece(m, c, turn)

    def take_slab(j1, j2):
        hh, lanes = slab_of(j1, j2, c)
        here = table.at[hh, :, lanes]
        arrived(here, slab_r.at[4 * j1 + j2])
        if j2 == 0:
            if j1 == 1:
                forward(here, here, 2, 0, step(1, 0))
            forward(here, here, j1, 1, step(0, 1))
            forward(here, here, j1, 3, step(0, 3))
        if j2 == 1 and j1 in (0, 1):
            forward(here, here, j1, 2, step(0, 1))
        if j2 == 3 and j1 in (2, 3):
            forward(here, here, j1, 2, step(0, 3))
        to_other_core(4 * j1 + j2, table.at[hh, third(o), lanes], (hh, lanes))
        split(table[hh, 0:256, lanes], pl.ds(pl.multiple_of(256 * hh, 256), 256), lanes)
        split_third(table[hh, third(c), lanes], hh, c, lanes)

    take_slab(1, 0)
    take_slab(3, 0)
    take_piece(1)
    take_piece(5)
    take_slab(0, 1)
    take_slab(0, 3)
    take_slab(2, 0)
    take_slab(1, 1)
    take_slab(3, 3)
    take_piece(2)
    take_piece(6)
    take_slab(1, 3)
    take_slab(3, 1)
    take_slab(2, 3)
    take_slab(2, 1)
    take_slab(0, 2)
    take_piece(3)
    take_piece(7)
    take_slab(1, 2)
    take_slab(3, 2)
    take_slab(2, 2)
    take_piece(4)

    @pl.when(native)
    def _():
        for n in range(2):
            arrived(piece(0, n, c, turn), swap_r.at[n])

    split_piece(0, c, turn)
    for m in (0, 1, 5, 2, 6, 3, 7, 4):
        for n in range(2):
            arrived(piece(m, n, o, 8 - turn), ringx_r.at[2 * m + n])
        split_piece(m, o, 8 - turn)
    for j1 in range(4):
        for j2 in range(4):
            hh, lanes = slab_of(j1, j2, o)
            arrived(extra.at[hh, :, lanes], slabx_r.at[4 * j1 + j2])
            split_third(extra[hh, :, lanes], hh, o, lanes)
    arrived(other_weight, half_r.at[2])

    def drain():
        for copy in to_sibling + lined + rings + across + slabs + first[0] + first[1]:
            copy.wait_send()

        @pl.when(jnp.logical_not(native))
        def _():
            for copy in swap:
                copy.wait_send()

    return drain


def kernel_values(spots, feats_hi, feats_lo, rows_hi, rows_lo, kp, kt, kp_s, kp_r, kt_s, kt_r):
    e, p, x, y, z, c = spots
    sibling = device(x, y, z, 1 - c)

    def values(rows, lanes):
        scaled = dot3((rows_hi[rows], rows_lo[rows]), (feats_hi[:, lanes], feats_lo[:, lanes]), ((1,), (0,))) * (1.0 / 32.0)
        return 0.25 * scaled * scaled * scaled

    sent = []

    def exchange(t):
        lanes = pl.ds(256 * t, 256)
        lead, trail = kp.at[:, :, c, :, lanes], kt.at[0:2, :, c, :, lanes]
        sent.append(remote(lead, lead, kp_s.at[t], kp_r.at[t], sibling))
        sent.append(remote(trail, trail, kt_s.at[t], kt_r.at[t], sibling))
        sent[-2].start()
        sent[-1].start()

    for t in range(4):
        lanes = pl.ds(256 * t, 256)
        value = values(pl.ds(0, 512), lanes)
        for hh in range(2):
            kp[hh, :, c, :, lanes] = value[256 * hh : 256 * hh + 128].reshape(8, 16, 256)
            kt[0:2, hh, c, :, lanes] = value[256 * hh + 128 : 256 * hh + 256].reshape(2, 64, 256)
        if t > 0:
            exchange(t - 1)
    for t in range(2):
        lanes = pl.ds(512 * t, 512)
        value = values(pl.ds(512, 256), lanes)
        kt[2, :, :, :, lanes] = value.reshape(2, 2, 64, 512)
        if t == 0:
            exchange(3)
    for t in range(4):
        lanes = pl.ds(256 * t, 256)
        arrived(kp.at[:, :, 1 - c, :, lanes], kp_r.at[t])
        arrived(kt.at[0:2, :, 1 - c, :, lanes], kt_r.at[t])

    def drain():
        for copy in sent:
            copy.wait_send()

    return drain


def multiply(spots, weight, other_weight, kp, kt, tt_out, panel_out, corner_out, send_corner):
    e, p, x, y, z, c = spots
    native = c == p // 8
    w = jnp.where(native, weight[0:1], other_weight[0:1]) * (1.0 / NENV)
    nt = ((1,), (1,))

    def unit(k, carry):
        first = (k + 1) // 2
        row = jnp.where(first == 1, c, 0)
        col = jnp.where(first == 0, 0, jnp.where(first == 1, 1 + c, 2))
        side = jnp.where(first == 0, c, (k + 1) % 2)
        a = halves(kt[row].reshape(256, 1024) * w)
        b = halves(kt[col, side].reshape(128, 1024))
        tt_out[k] = dot3(a, b, nt)
        return carry

    trail = halves(kt[0, c].reshape(128, 1024) * w)
    lead = halves(kp[c, z].reshape(32, 1024) * w)

    def panel(i, carry):
        a = halves(kp[i // 2, pl.ds(4 * (i % 2), 4)].reshape(128, 1024))
        corner_out[i] = dot3(lead, a, nt)
        panel_out[pl.ds(4 * i, 4)] = dot3(a, trail, nt).reshape(4, 32, 128)
        return carry

    lax.fori_loop(0, 4, panel, 0)
    send_corner()
    lax.fori_loop(0, 5, unit, 0)


def dot_hi(a, b, dims):
    return dot3(halves(a), halves(b), dims)


def inverse_factor(d_ref, e_ref):
    rows = lax.broadcasted_iota(jnp.int32, (8, NB), 0)
    lanes = lax.broadcasted_iota(jnp.int32, (8, NB), 1)
    groups = NB // 8
    full = lambda v: jnp.broadcast_to(v, (8, NB))
    for g in range(groups):
        e_ref[8 * g : 8 * g + 8, :] = (lanes == rows + 8 * g).astype(F32)
    for t in range(groups):
        v = d_ref[8 * t : 8 * t + 8, :]
        e = e_ref[8 * t : 8 * t + 8, :]
        c = [full(v[:, 8 * t + i : 8 * t + i + 1]) for i in range(8)]
        v_row, e_row, c_row, inv = [], [], [], []
        pivots = jnp.ones((8, NB), F32)
        for i in range(8):
            pivot = full(c[i][i : i + 1])
            pivots = jnp.where(rows == i, pivot, pivots)
            r = 1.0 / pivot
            inv.append(r)
            v_row.append(full(v[i : i + 1]))
            e_row.append(full(e[i : i + 1]))
            c_row.append([full(c[k][i : i + 1]) if k > i else None for k in range(8)])
            if i < 7:
                low = jnp.where(rows > i, c[i], 0.0)
                m = low * r
                c[i + 1] = c[i + 1] - (low * c_row[i][i + 1]) * r
                for k in range(i + 2, 8):
                    c[k] = c[k] - m * c_row[i][k]
                v = v - m * v_row[i]
                e = e - m * e_row[i]
        e_ref[8 * t : 8 * t + 8, :] = e * lax.rsqrt(pivots)
        for g in range(t + 1, groups):
            v = d_ref[8 * g : 8 * g + 8, :]
            e = e_ref[8 * g : 8 * g + 8, :]
            c = [full(v[:, 8 * t + i : 8 * t + i + 1]) for i in range(8)]
            for i in range(8):
                m = c[i] * inv[i]
                for k in range(i + 1, 8):
                    c[k] = c[k] - m * c_row[i][k]
                v = v - m * v_row[i]
                e = e - m * e_row[i]
            d_ref[8 * g : 8 * g + 8, :] = v
            e_ref[8 * g : 8 * g + 8, :] = e


def whole(
    desc, points_t, weight, panel_ref, trail_ref,
    points, half, other_weight, line, table, extra, feats, feats_hi, feats_lo, rows_hi, rows_lo, kp, kt, tt, pp, cc,
    c_in, c_z, c_all, p_in, p_rows, p_cols, t_own, tt_in, tt_own, block, a, ui, uj, d, inv_ref,
    half_s, half_r, swap_s, swap_r, zp_s, zp_r, zt_s, zt_r, slab_s, slab_r, slabx_s, slabx_r,
    ring_s, ring_r, ringx_s, ringx_r, kp_s, kp_r, kt_s, kt_r,
    c_s, c_r, cz_s, cz_r, cp_s, cp_r, cx_s, cx_r, keep_s,
    p_s, p_r, tt_s, tt_r, col_s, col_r, row_s, row_r, blk_s, blk_r,
):
    spots = placed()
    e, p, x, y, z, c = spots
    h = p // 8
    me = 4 * x + y
    sibling = device(x, y, z, 1 - c)
    in_plane = lambda q: device((x + q // 4) % 4, (y + q % 4) % 4, z, c)
    index_at = lambda q: 4 * ((x + q // 4) % 4) + (y + q % 4) % 4
    index_from = lambda q: 4 * ((x + 4 - q // 4) % 4) + (y + 4 - q % 4) % 4
    along_z = lambda q: device(x, y, (z + q) % 8, c)
    barrier = pltpu.get_barrier_semaphore()

    def is_me(to):
        return (to[0] == e) & (to[1] == p)

    def send(src, dst, send_sem, recv_sem, to, also=None):
        here, there = is_me(to), jnp.logical_not(is_me(to))
        if also is not None:
            here, there = here & also, there & also

        @pl.when(here)
        def _():
            pltpu.make_async_copy(src, dst, recv_sem).start()

        @pl.when(there)
        def _():
            remote(src, dst, send_sem, recv_sem, to).start()

        def finish():
            @pl.when(there)
            def _():
                remote(src, dst, send_sem, recv_sem, to).wait_send()

        return finish

    z_row, z_col = e % 8, z
    apart = (z_col + 8 - z_row) % 8
    straight = apart <= 4
    owners = []
    for k in range(5):
        first = (k + 1) // 2
        d_row = c if first == 1 else 0
        d_col = (0, 1 + 3 * c, 2 + 2 * c)[first]
        side = c if k == 0 else (k + 1) % 2
        p_a = 8 * (me // 8) + (z + d_row) % 8
        p_b = 8 * side + (z + d_col) % 8
        owners.append((2 * k, k, (p_a, p_b), None))
        if k > 0:
            owners.append((2 * k + 1, k, (p_b, p_a), None if first == 1 else c == 0))

    pl.semaphore_signal(barrier, inc=1, device_id=sibling, device_id_type=MESH)
    pl.semaphore_signal(barrier, inc=1, device_id=device(x, (y + 2) % 4, z, 1 - c), device_id_type=MESH)
    for q in range(1, 16):
        pl.semaphore_signal(barrier, inc=1, device_id=in_plane(q), device_id_type=MESH)
    for q in range(1, 8):
        pl.semaphore_signal(barrier, inc=1, device_id=along_z(q), device_id_type=MESH)
    points[...] = jnp.transpose(points_t[...])
    pl.semaphore_wait(barrier, 24)

    drain = gather(
        spots, desc, points, weight, half, other_weight, line, table, extra, feats, feats_hi, feats_lo, rows_hi, rows_lo,
        half_s, half_r, swap_s, swap_r, zp_s, zp_r, zt_s, zt_r, slab_s, slab_r, slabx_s, slabx_r,
        ring_s, ring_r, ringx_s, ringx_r,
    )
    drain_values = kernel_values(spots, feats_hi, feats_lo, rows_hi, rows_lo, kp, kt, kp_s, kp_r, kt_s, kt_r)
    pending, plain = [], []

    def go(copy):
        copy.start()
        plain.append(copy)

    def corner_rows(q):
        return pl.ds(pl.multiple_of(8 * (q // 4), 8), 8)

    def send_corner():
        stay = pltpu.make_async_copy(cc.at[me % 4, corner_rows(me)], c_in.at[me], c_r.at[0])
        stay.start()
        for q in range(1, 16):
            there = index_at(q)
            go(remote(cc.at[there % 4, corner_rows(there)], c_in.at[me], c_s.at[q], c_r.at[q], in_plane(q)))

    multiply(spots, weight, other_weight, kp, kt, tt, pp, cc, send_corner)

    for q in range(16):
        arrived(c_in.at[index_from(q)], c_r.at[q])
    total = c_in[0]
    for q in range(1, 16):
        total = total + c_in[q]
    at_row = 256 * c + 32 * z + 8 * (me // 4) + lax.broadcasted_iota(jnp.int32, (8, 128), 0)
    at_col = 128 * (me % 4) + lax.broadcasted_iota(jnp.int32, (8, 128), 1)
    c_z[z] = total + jnp.where(at_row == at_col, 1.0, 0.0)
    for q in range(1, 8):
        go(remote(c_z.at[z], c_z.at[z], cz_s.at[q], cz_r.at[q], along_z(q)))
    pending.append(send(pp.at[e], p_in.at[me], p_s.at[0], p_r.at[me], (e, 8 * c + z)))
    for q in range(1, 16):
        go(remote(pp.at[(e + q) % 16], p_in.at[me], p_s.at[q], p_r.at[me], ((e + q) % 16, 8 * c + z)))
    for q in range(1, 8):
        arrived(c_z.at[(z + 8 - q) % 8], cz_r.at[q])

    def corner_part(q, core):
        return c_all.at[core, :, q // 4, :, pl.ds(pl.multiple_of(128 * (q % 4), 128), 128)]

    def near(j1, j2):
        return (x + j1 * (1 - c) + j2 * c) % 4, (y + j1 * c + j2 * (1 - c)) % 4

    def origin(j1, j2, core):
        sx = (x + 8 - j1 * (1 - core) - j2 * core) % 4
        sy = (y + 8 - j1 * core - j2 * (1 - core)) % 4
        return 4 * sx + sy

    for j in (1, 3, 2):
        go(remote(c_z, corner_part(me, c), cp_s.at[4 * j], cp_r.at[4 * j], device(*near(j, 0), z, c)))
    for j in (1, 3, 2):
        go(remote(c_z, corner_part(me, c), cp_s.at[j], cp_r.at[j], device(*near(0, j), z, c)))
    go(remote(c_z, corner_part(me, c), cx_s.at[0], cx_r.at[0], sibling))
    keep = pltpu.make_async_copy(c_z, corner_part(me, c), keep_s)
    keep.start()

    for j1, j2 in [(j, 0) for j in (1, 3, 2)] + [(0, j) for j in (1, 3, 2)] + [(k, j) for k in (1, 3, 2) for j in (1, 3, 2)]:
        q = 4 * j1 + j2
        part = corner_part(origin(j1, j2, c), c)
        arrived(part, cp_r.at[q])
        if j2 == 0:
            for j in (1, 3, 2):
                go(remote(part, part, cp_s.at[q + j], cp_r.at[q + j], device(*near(0, j), z, c)))
        go(remote(part, part, cx_s.at[q], cx_r.at[q], sibling))
    for q in range(16):
        arrived(p_in.at[q], p_r.at[q])
    total = p_in[0]
    for q in range(1, 16):
        total = total + p_in[q]
    t_own[...] = total
    pending.append(send(t_own, p_rows.at[e], row_s.at[0], row_r.at[e], (p, p)))
    pending.append(send(t_own, p_cols.at[e], col_s.at[0], col_r.at[e], (e, p)))
    for q in range(1, 16):
        go(remote(t_own, p_rows.at[e], row_s.at[q], row_r.at[e], (p, (p + q) % 16)))
        go(remote(t_own, p_cols.at[e], col_s.at[q], col_r.at[e], ((e + q) % 16, p)))
    stay_tt = pltpu.make_async_copy(tt.at[:, pl.ds(pl.multiple_of(16 * me, 16), 16)], tt_in.at[me], tt_r.at[me])
    stay_tt.start()
    for q in range(1, 16):
        rows = pl.ds(pl.multiple_of(16 * index_at(q), 16), 16)
        go(remote(tt.at[:, rows], tt_in.at[me], tt_s.at[q], tt_r.at[me], in_plane(q)))
    keep.wait()
    for q in range(16):
        arrived(corner_part(origin(q // 4, q % 4, 1 - c), 1 - c), cx_r.at[q])

    n = a.shape[0]
    a[...] = c_all[...].reshape(n, n)
    ui[:, 128:256] = a[:, pl.ds(pl.multiple_of(128 * (e // 4), 128), 128)]
    def apply(k):
        lo, hi = k * NB, (k + 1) * NB
        inv = inv_ref[k]
        ui[lo:hi, :] = dot_hi(inv, ui[lo:hi, :], ((1,), (0,)))
        uj[lo:hi, :] = dot_hi(inv, uj[lo:hi, :], ((1,), (0,)))
        if hi < n:
            u = a[lo:hi, hi:]
            ui[hi:, :] -= dot_hi(u, ui[lo:hi, :], ((0,), (0,)))
            uj[hi:, :] -= dot_hi(u, uj[lo:hi, :], ((0,), (0,)))

    for k in range(n // NB):
        lo, hi = k * NB, (k + 1) * NB
        d[...] = a[lo:hi, lo:hi]
        inverse_factor(d, inv_ref.at[k])
        if k >= 2:
            apply(k - 1)
        if hi < n:
            a[lo:hi, hi:] = dot_hi(inv_ref[k], a[lo:hi, hi:], ((1,), (0,)))
            u = a[lo:hi, hi:]
            a[hi:, hi:] -= dot_hi(u, u, ((0,), (0,)))
        if k == 1:
            for q in range(16):
                arrived(tt_in.at[q], tt_r.at[q])
            total = tt_in[0]
            for q in range(1, 16):
                total = total + tt_in[q]
            tt_own[...] = total
            part = me % 8
            rows = pl.ds(pl.multiple_of(16 * part, 16), 16)
            for m, kk, to, also in owners:
                pending.append(send(tt_own.at[kk], block.at[rows], blk_s.at[m], blk_r.at[part], to, also))
            for q in range(16):
                arrived(p_rows.at[q], row_r.at[q])
                arrived(p_cols.at[q], col_r.at[q])
            ui[:, 0:128] = p_rows[...].reshape(n, 128)
            uj[...] = p_cols[...].reshape(n, 128)
            apply(0)
    apply(n // NB - 1)
    for t in range(8):
        arrived(block.at[16 * t : 16 * t + 16], blk_r.at[t])
    gram = block[...]
    gram = jnp.where(straight, gram, jnp.transpose(gram))
    same = lax.broadcasted_iota(jnp.int32, (128, 128), 0) == lax.broadcasted_iota(jnp.int32, (128, 128), 1)
    gram = gram + jnp.where(same & (e == p), 1.0, 0.0)
    trail_ref[...] = gram - dot_hi(ui[:, 0:128], uj[...], ((0,), (0,)))
    own_rows = ui[pl.ds(pl.multiple_of(32 * p, 32), 32), :]
    lead = pltpu.roll(own_rows[:, 128:256], (128 - 32 * (e % 4)) % 128, 1)
    rest = pltpu.roll(own_rows[:, 0:128], 32, 1)
    lanes = lax.broadcasted_iota(jnp.int32, (32, 128), 1)
    panel_ref[:, 0:128] = jnp.where(lanes < 32, lead, rest)
    panel_ref[:, 128:160] = rest[:, 0:32]
    for copy in plain:
        copy.wait_send()
    for finish in pending:
        finish()
    drain()
    drain_values()


def fit(desc, points_t, weight):
    dma = pltpu.SemaphoreType.DMA
    vmem = pl.BlockSpec(memory_space=pltpu.VMEM)
    f32 = lambda *shape: pltpu.VMEM(shape, F32)
    bf16 = lambda *shape: pltpu.VMEM(shape, BF16)
    return pl.pallas_call(
        whole,
        out_shape=(jax.ShapeDtypeStruct((32, 160), F32), jax.ShapeDtypeStruct((128, 128), F32)),
        in_specs=[vmem] * 3,
        out_specs=[vmem] * 2,
        scratch_shapes=[
            f32(160, 64), f32(80, 64), f32(1, 1024), f32(384, 128), f32(2, 384, 1024), f32(2, 64, 1024), f32(16, 64, 1024),
            bf16(1024, 1024), bf16(1024, 1024), bf16(768, 1024), bf16(768, 1024),
            f32(2, 8, 2, 16, 1024), f32(3, 2, 2, 64, 1024), f32(5, 256, 128), f32(16, 32, 128), f32(4, 32, 128),
            f32(16, 8, 128), f32(8, 8, 128), f32(2, 8, 4, 8, 512), f32(16, 32, 128), f32(16, 32, 128), f32(16, 32, 128),
            f32(32, 128), f32(16, 5, 16, 128), f32(5, 16, 128), f32(128, 128),
            f32(512, 512), f32(512, 256), f32(512, 128), f32(NB, NB), f32(4, NB, NB),
            dma((3,)), dma((3,)), dma((2,)), dma((2,)),
            dma((8,)), dma((8,)), dma((4,)), dma((4,)),
            dma((16,)), dma((16,)), dma((16,)), dma((16,)),
            dma((16,)), dma((16,)), dma((16,)), dma((16,)),
            dma((4,)), dma((4,)), dma((4,)), dma((4,)),
        ]
        + [dma((16,))] * 8
        + [dma]
        + [dma((16,))] * 10,
        compiler_params=pltpu.CompilerParams(collective_id=0, has_side_effects=True, vmem_limit_bytes=60 * 2**20),
    )(desc, points_t, weight)


def local(descriptors, env_weight, points):
    panel_t, trailing = fit(descriptors, points.T, env_weight.reshape(1, -1))
    return panel_t.T, trailing


def solution(mesh):
    return jax.shard_map(
        local,
        mesh=mesh,
        in_specs=(P("pts", "env"), P("env"), P("pts", "env")),
        out_specs=(P("env", "pts"), P("env", "pts")),
        check_vma=False,
    )
```

```python
import functools

import jax
import jax.numpy as jnp
from jax import lax
from jax.experimental import pallas as pl
from jax.experimental.pallas import tpu as pltpu
from jax.sharding import PartitionSpec as P

MESH = pl.DeviceIdType.MESH
HI = lax.Precision.HIGHEST
F32 = jnp.float32
BF16 = jnp.bfloat16
NB = 128
NENV = 16384
OFFSETS = (0, 1, 2, 4)


def placed():
    e, p = lax.axis_index("env"), lax.axis_index("pts")
    x, y_lo, c = e // 4, (e // 2) % 2, e % 2
    y_hi, z = p // 8, p % 8
    return e, p, x, 2 * y_hi + y_lo, z, c


def device(x, y, z, c):
    return (4 * x + 2 * (y % 2) + c, 8 * (y // 2) + z)


def remote(src, dst, send_sem, recv_sem, to):
    return pltpu.make_async_remote_copy(
        src_ref=src, dst_ref=dst, send_sem=send_sem, recv_sem=recv_sem, device_id=to, device_id_type=MESH
    )


def arrived(ref, sem):
    pltpu.make_async_copy(ref, ref, sem).wait()


def halves(a):
    hi = a.astype(BF16)
    return hi, (a - hi.astype(F32)).astype(BF16)


def dot3(a, b, dims):
    one = lambda l, r: lax.dot_general(l, r, (dims, ((), ())), preferred_element_type=F32)
    return one(a[0], b[0]) + (one(a[0], b[1]) + one(a[1], b[0]))


def gather(
    spots, desc, points, weight,
    half, other_weight, line, table, extra, feats, feats_hi, feats_lo, rows_hi, rows_lo,
    half_s, half_r, swap_s, swap_r, zp_s, zp_r, zt_s, zt_r, slab_s, slab_r, slabx_s, slabx_r,
    ring_s, ring_r, ringx_s, ringx_r,
):
    e, p, x, y, z, c = spots
    h = p // 8
    native = c == h
    turn = jnp.where(native, 1, 7)
    sibling = device(x, y, z, 1 - c)
    partner = device(x, (y + 2) % 4, z, 1 - c)
    along_z = lambda d: device(x, y, (z + d) % 8, c)

    def step(j1, j2):
        return (x + j1 * (1 - c) + j2 * c) % 4, (y + j1 * c + j2 * (1 - c)) % 4

    def slab_of(j1, j2, core):
        sx = (x + 8 - j1 * (1 - core) - j2 * core) % 4
        sy = (y + 8 - j1 * core - j2 * (1 - core)) % 4
        lanes = pl.multiple_of(128 * (2 * sx + sy % 2), 128)
        return sy // 2, pl.ds(lanes, 128)

    o = 1 - c
    to_sibling = [
        remote(points.at[pl.ds(pl.multiple_of(16 * o, 16), 16)], half.at[0:16], half_s.at[0], half_r.at[0], sibling),
        remote(points.at[pl.ds(pl.multiple_of(32 + 64 * o, 32), 64)], half.at[16:80], half_s.at[1], half_r.at[1], sibling),
        remote(weight, other_weight, half_s.at[2], half_r.at[2], sibling),
    ]
    for copy in to_sibling:
        copy.start()
    parts = [pl.ds(32 * n, 32) for n in range(2)]
    swap = [remote(desc.at[r], feats.at[p, r], swap_s.at[n], swap_r.at[n], partner) for n, r in enumerate(parts)]
    keep = [pltpu.make_async_copy(desc.at[r], feats.at[p, r], swap_r.at[n]) for n, r in enumerate(parts)]

    def piece(m, n, core, sign):
        d = (0, 1, 2, 3, 4, 7, 6, 5)[m]
        return feats.at[8 * core + (z + 8 * 8 - sign * d) % 8, parts[n]]

    def first_sends(src, n):
        dst = piece(0, n, c, turn)
        return [
            remote(src, dst, ring_s.at[2 + n], ring_r.at[2 + n], along_z(turn)),
            remote(src, dst, ring_s.at[10 + n], ring_r.at[10 + n], along_z(8 - turn)),
            remote(src, dst, ringx_s.at[n], ringx_r.at[n], sibling),
        ]

    first = [first_sends(piece(0, n, c, turn), n) for n in range(2)]

    @pl.when(native)
    def _():
        for n in range(2):
            for copy in first_sends(desc.at[parts[n]], n):
                copy.start()
        for copy in keep:
            copy.start()

    @pl.when(jnp.logical_not(native))
    def _():
        for copy in swap:
            copy.start()

    arrived(half.at[0:16], half_r.at[0])
    arrived(half.at[16:80], half_r.at[1])
    mine = jnp.concatenate(
        [points[pl.ds(pl.multiple_of(16 * c, 16), 16)], points[pl.ds(pl.multiple_of(32 + 64 * c, 32), 64)]], axis=0
    )
    theirs = half[...]
    packed = jnp.where(c == 0, jnp.concatenate([mine, theirs], axis=1), jnp.concatenate([theirs, mine], axis=1))
    own_panel = line.at[pl.ds(pl.multiple_of(16 * z, 16), 16)]
    line[pl.ds(pl.multiple_of(16 * z, 16), 16)] = packed[0:16]
    line[128:192] = packed[16:80]

    lined = []
    for s in (1, 2, 3):
        rows = pl.ds(128 + 64 * s, 64)
        lined.append(remote(line.at[128:192], line.at[rows], zt_s.at[s], zt_r.at[s], along_z(8 - OFFSETS[s])))
    for d in range(1, 8):
        lined.append(remote(own_panel, own_panel, zp_s.at[d], zp_r.at[d], along_z(d)))
    for copy in lined:
        copy.start()

    rings, across = [], []

    def pass_on(m, n):
        src = piece(m, n, c, turn)
        if m in (1, 2, 3):
            at = 2 * (m + 1) + n
            rings.append(remote(src, src, ring_s.at[at], ring_r.at[at], along_z(turn)))
            rings[-1].start()
        if m in (5, 6):
            at = 2 * (m + 1) + n
            rings.append(remote(src, src, ring_s.at[at], ring_r.at[at], along_z(8 - turn)))
            rings[-1].start()
        at = 2 * m + n
        across.append(remote(src, src, ringx_s.at[at], ringx_r.at[at], sibling))
        across[-1].start()

    @pl.when(jnp.logical_not(native))
    def _():
        for n in range(2):
            arrived(piece(0, n, c, turn), swap_r.at[n])
            for copy in first[n]:
                copy.start()

    for s in (1, 2, 3):
        arrived(line.at[pl.ds(128 + 64 * s, 64)], zt_r.at[s])
    for d in range(1, 8):
        rows = pl.ds(pl.multiple_of(16 * ((z + 8 - d) % 8), 16), 16)
        arrived(line.at[rows], zp_r.at[d])

    slabs = []

    def forward(src, dst, j1, j2, to):
        n = 4 * j1 + j2
        slabs.append(remote(src, dst, slab_s.at[n], slab_r.at[n], device(*to, z, c)))
        slabs[-1].start()

    def third(core):
        return pl.ds(pl.multiple_of(256 + 64 * core, 64), 64)

    def to_other_core(n, src, at):
        slabs.append(remote(src, extra.at[at[0], :, at[1]], slabx_s.at[n], slabx_r.at[n], sibling))
        slabs[-1].start()

    def split(value, rows, lanes):
        hi, lo = halves(value)
        rows_hi[rows, lanes] = hi
        rows_lo[rows, lanes] = lo

    def split_third(value, hh, cc, lanes):
        split(value, pl.ds(pl.multiple_of(512 + 128 * hh + 64 * cc, 64), 64), lanes)

    def split_piece(m, core, sign):
        d = (0, 1, 2, 3, 4, 7, 6, 5)[m]
        slot = 8 * core + (z + 8 * 8 - sign * d) % 8
        hi, lo = halves(feats[slot])
        at = pl.ds(pl.multiple_of(64 * slot, 64), 64)
        feats_hi[at] = hi
        feats_lo[at] = lo

    mine_h, mine_lanes = slab_of(0, 0, c)
    own = table.at[mine_h, :, mine_lanes]
    forward(line, own, 1, 0, step(1, 0))
    forward(line, own, 3, 0, step(3, 0))
    forward(line, own, 0, 1, step(0, 1))
    forward(line, own, 0, 3, step(0, 3))
    to_other_core(0, line.at[third(o)], (mine_h, mine_lanes))
    split(line[0:256], pl.ds(pl.multiple_of(256 * mine_h, 256), 256), mine_lanes)
    split_third(line[third(c)], mine_h, c, mine_lanes)

    def take_piece(m):
        for n in range(2):
            arrived(piece(m, n, c, turn), ring_r.at[2 * m + n])
            pass_on(m, n)
        split_piece(m, c, turn)

    def take_slab(j1, j2):
        hh, lanes = slab_of(j1, j2, c)
        here = table.at[hh, :, lanes]
        arrived(here, slab_r.at[4 * j1 + j2])
        if j2 == 0:
            if j1 == 1:
                forward(here, here, 2, 0, step(1, 0))
            forward(here, here, j1, 1, step(0, 1))
            forward(here, here, j1, 3, step(0, 3))
        if j2 == 1 and j1 in (0, 1):
            forward(here, here, j1, 2, step(0, 1))
        if j2 == 3 and j1 in (2, 3):
            forward(here, here, j1, 2, step(0, 3))
        to_other_core(4 * j1 + j2, table.at[hh, third(o), lanes], (hh, lanes))
        split(table[hh, 0:256, lanes], pl.ds(pl.multiple_of(256 * hh, 256), 256), lanes)
        split_third(table[hh, third(c), lanes], hh, c, lanes)

    take_slab(1, 0)
    take_slab(3, 0)
    take_piece(1)
    take_piece(5)
    take_slab(0, 1)
    take_slab(0, 3)
    take_slab(2, 0)
    take_slab(1, 1)
    take_slab(3, 3)
    take_piece(2)
    take_piece(6)
    take_slab(1, 3)
    take_slab(3, 1)
    take_slab(2, 3)
    take_slab(2, 1)
    take_slab(0, 2)
    take_piece(3)
    take_piece(7)
    take_slab(1, 2)
    take_slab(3, 2)
    take_slab(2, 2)
    take_piece(4)

    @pl.when(native)
    def _():
        for n in range(2):
            arrived(piece(0, n, c, turn), swap_r.at[n])

    split_piece(0, c, turn)
    for m in (0, 1, 5, 2, 6, 3, 7, 4):
        for n in range(2):
            arrived(piece(m, n, o, 8 - turn), ringx_r.at[2 * m + n])
        split_piece(m, o, 8 - turn)
    for j1 in range(4):
        for j2 in range(4):
            hh, lanes = slab_of(j1, j2, o)
            arrived(extra.at[hh, :, lanes], slabx_r.at[4 * j1 + j2])
            split_third(extra[hh, :, lanes], hh, o, lanes)
    arrived(other_weight, half_r.at[2])

    def drain():
        for copy in to_sibling + lined + rings + across + slabs + first[0] + first[1]:
            copy.wait_send()

        @pl.when(jnp.logical_not(native))
        def _():
            for copy in swap:
                copy.wait_send()

    return drain


def kernel_values(spots, feats_hi, feats_lo, rows_hi, rows_lo, kp, kt, kp_s, kp_r, kt_s, kt_r):
    e, p, x, y, z, c = spots
    sibling = device(x, y, z, 1 - c)

    def values(rows, lanes):
        scaled = dot3((rows_hi[rows], rows_lo[rows]), (feats_hi[:, lanes], feats_lo[:, lanes]), ((1,), (0,))) * (1.0 / 32.0)
        return 0.25 * scaled * scaled * scaled

    sent = []

    def exchange(t):
        lanes = pl.ds(256 * t, 256)
        lead, trail = kp.at[:, :, c, :, lanes], kt.at[0:2, :, c, :, lanes]
        sent.append(remote(lead, lead, kp_s.at[t], kp_r.at[t], sibling))
        sent.append(remote(trail, trail, kt_s.at[t], kt_r.at[t], sibling))
        sent[-2].start()
        sent[-1].start()

    for t in range(4):
        lanes = pl.ds(256 * t, 256)
        value = values(pl.ds(0, 512), lanes)
        for hh in range(2):
            kp[hh, :, c, :, lanes] = value[256 * hh : 256 * hh + 128].reshape(8, 16, 256)
            kt[0:2, hh, c, :, lanes] = value[256 * hh + 128 : 256 * hh + 256].reshape(2, 64, 256)
        if t > 0:
            exchange(t - 1)
    for t in range(2):
        lanes = pl.ds(512 * t, 512)
        value = values(pl.ds(512, 256), lanes)
        kt[2, :, :, :, lanes] = value.reshape(2, 2, 64, 512)
        if t == 0:
            exchange(3)
    for t in range(4):
        lanes = pl.ds(256 * t, 256)
        arrived(kp.at[:, :, 1 - c, :, lanes], kp_r.at[t])
        arrived(kt.at[0:2, :, 1 - c, :, lanes], kt_r.at[t])

    def drain():
        for copy in sent:
            copy.wait_send()

    return drain


def multiply(spots, weight, other_weight, kp, kt, tt_out, panel_out, corner_out, send_corner):
    e, p, x, y, z, c = spots
    native = c == p // 8
    w = jnp.where(native, weight[0:1], other_weight[0:1]) * (1.0 / NENV)
    nt = ((1,), (1,))

    def unit(k, carry):
        first = (k + 1) // 2
        row = jnp.where(first == 1, c, 0)
        col = jnp.where(first == 0, 0, jnp.where(first == 1, 1 + c, 2))
        side = jnp.where(first == 0, c, (k + 1) % 2)
        a = halves(kt[row].reshape(256, 1024) * w)
        b = halves(kt[col, side].reshape(128, 1024))
        tt_out[k] = dot3(a, b, nt)
        return carry

    trail = halves(kt[0, c].reshape(128, 1024) * w)
    lead = halves(kp[c, z].reshape(32, 1024) * w)

    def panel(i, carry):
        a = halves(kp[i // 2, pl.ds(4 * (i % 2), 4)].reshape(128, 1024))
        corner_out[i] = dot3(lead, a, nt)
        panel_out[pl.ds(4 * i, 4)] = dot3(a, trail, nt).reshape(4, 32, 128)
        return carry

    lax.fori_loop(0, 4, panel, 0)
    send_corner()
    lax.fori_loop(0, 5, unit, 0)


def dot_hi(a, b, dims):
    return dot3(halves(a), halves(b), dims)


def inverse_factor(d_ref, e_ref):
    rows = lax.broadcasted_iota(jnp.int32, (8, NB), 0)
    lanes = lax.broadcasted_iota(jnp.int32, (8, NB), 1)
    groups = NB // 8
    full = lambda v: jnp.broadcast_to(v, (8, NB))
    for g in range(groups):
        e_ref[8 * g : 8 * g + 8, :] = (lanes == rows + 8 * g).astype(F32)
    for t in range(groups):
        v = d_ref[8 * t : 8 * t + 8, :]
        e = e_ref[8 * t : 8 * t + 8, :]
        c = [full(v[:, 8 * t + i : 8 * t + i + 1]) for i in range(8)]
        v_row, e_row, c_row, inv = [], [], [], []
        pivots = jnp.ones((8, NB), F32)
        for i in range(8):
            pivot = full(c[i][i : i + 1])
            pivots = jnp.where(rows == i, pivot, pivots)
            r = 1.0 / pivot
            inv.append(r)
            v_row.append(full(v[i : i + 1]))
            e_row.append(full(e[i : i + 1]))
            c_row.append([full(c[k][i : i + 1]) if k > i else None for k in range(8)])
            if i < 7:
                low = jnp.where(rows > i, c[i], 0.0)
                m = low * r
                c[i + 1] = c[i + 1] - (low * c_row[i][i + 1]) * r
                for k in range(i + 2, 8):
                    c[k] = c[k] - m * c_row[i][k]
                v = v - m * v_row[i]
                e = e - m * e_row[i]
        e_ref[8 * t : 8 * t + 8, :] = e * lax.rsqrt(pivots)
        for g in range(t + 1, groups):
            v = d_ref[8 * g : 8 * g + 8, :]
            e = e_ref[8 * g : 8 * g + 8, :]
            c = [full(v[:, 8 * t + i : 8 * t + i + 1]) for i in range(8)]
            for i in range(8):
                m = c[i] * inv[i]
                for k in range(i + 1, 8):
                    c[k] = c[k] - m * c_row[i][k]
                v = v - m * v_row[i]
                e = e - m * e_row[i]
            d_ref[8 * g : 8 * g + 8, :] = v
            e_ref[8 * g : 8 * g + 8, :] = e


def whole(
    desc, points_t, weight, panel_ref, trail_ref,
    points, half, other_weight, line, table, extra, feats, feats_hi, feats_lo, rows_hi, rows_lo, kp, kt, tt, pp, cc,
    c_in, c_z, c_all, p_in, p_rows, p_cols, t_own, tt_in, tt_own, block, a, ui, uj, d, inv_ref,
    half_s, half_r, swap_s, swap_r, zp_s, zp_r, zt_s, zt_r, slab_s, slab_r, slabx_s, slabx_r,
    ring_s, ring_r, ringx_s, ringx_r, kp_s, kp_r, kt_s, kt_r,
    c_s, c_r, cz_s, cz_r, cp_s, cp_r, cx_s, cx_r, keep_s,
    p_s, p_r, tt_s, tt_r, col_s, col_r, row_s, row_r, blk_s, blk_r,
):
    spots = placed()
    e, p, x, y, z, c = spots
    h = p // 8
    me = 4 * x + y
    sibling = device(x, y, z, 1 - c)
    in_plane = lambda q: device((x + q // 4) % 4, (y + q % 4) % 4, z, c)
    index_at = lambda q: 4 * ((x + q // 4) % 4) + (y + q % 4) % 4
    index_from = lambda q: 4 * ((x + 4 - q // 4) % 4) + (y + 4 - q % 4) % 4
    along_z = lambda q: device(x, y, (z + q) % 8, c)
    barrier = pltpu.get_barrier_semaphore()

    def is_me(to):
        return (to[0] == e) & (to[1] == p)

    def send(src, dst, send_sem, recv_sem, to, also=None):
        here, there = is_me(to), jnp.logical_not(is_me(to))
        if also is not None:
            here, there = here & also, there & also

        @pl.when(here)
        def _():
            pltpu.make_async_copy(src, dst, recv_sem).start()

        @pl.when(there)
        def _():
            remote(src, dst, send_sem, recv_sem, to).start()

        def finish():
            @pl.when(there)
            def _():
                remote(src, dst, send_sem, recv_sem, to).wait_send()

        return finish

    z_row, z_col = e % 8, z
    apart = (z_col + 8 - z_row) % 8
    straight = apart <= 4
    owners = []
    for k in range(5):
        first = (k + 1) // 2
        d_row = c if first == 1 else 0
        d_col = (0, 1 + 3 * c, 2 + 2 * c)[first]
        side = c if k == 0 else (k + 1) % 2
        p_a = 8 * (me // 8) + (z + d_row) % 8
        p_b = 8 * side + (z + d_col) % 8
        owners.append((2 * k, k, (p_a, p_b), None))
        if k > 0:
            owners.append((2 * k + 1, k, (p_b, p_a), None if first == 1 else c == 0))

    pl.semaphore_signal(barrier, inc=1, device_id=sibling, device_id_type=MESH)
    pl.semaphore_signal(barrier, inc=1, device_id=device(x, (y + 2) % 4, z, 1 - c), device_id_type=MESH)
    for q in range(1, 16):
        pl.semaphore_signal(barrier, inc=1, device_id=in_plane(q), device_id_type=MESH)
    for q in range(1, 8):
        pl.semaphore_signal(barrier, inc=1, device_id=along_z(q), device_id_type=MESH)
    points[...] = jnp.transpose(points_t[...])
    pl.semaphore_wait(barrier, 24)

    drain = gather(
        spots, desc, points, weight, half, other_weight, line, table, extra, feats, feats_hi, feats_lo, rows_hi, rows_lo,
        half_s, half_r, swap_s, swap_r, zp_s, zp_r, zt_s, zt_r, slab_s, slab_r, slabx_s, slabx_r,
        ring_s, ring_r, ringx_s, ringx_r,
    )
    drain_values = kernel_values(spots, feats_hi, feats_lo, rows_hi, rows_lo, kp, kt, kp_s, kp_r, kt_s, kt_r)
    pending, plain = [], []

    def go(copy):
        copy.start()
        plain.append(copy)

    def corner_rows(q):
        return pl.ds(pl.multiple_of(8 * (q // 4), 8), 8)

    def send_corner():
        stay = pltpu.make_async_copy(cc.at[me % 4, corner_rows(me)], c_in.at[me], c_r.at[0])
        stay.start()
        for q in range(1, 16):
            there = index_at(q)
            go(remote(cc.at[there % 4, corner_rows(there)], c_in.at[me], c_s.at[q], c_r.at[q], in_plane(q)))

    multiply(spots, weight, other_weight, kp, kt, tt, pp, cc, send_corner)

    for q in range(16):
        arrived(c_in.at[index_from(q)], c_r.at[q])
    total = c_in[0]
    for q in range(1, 16):
        total = total + c_in[q]
    at_row = 256 * c + 32 * z + 8 * (me // 4) + lax.broadcasted_iota(jnp.int32, (8, 128), 0)
    at_col = 128 * (me % 4) + lax.broadcasted_iota(jnp.int32, (8, 128), 1)
    c_z[z] = total + jnp.where(at_row == at_col, 1.0, 0.0)
    for q in range(1, 8):
        go(remote(c_z.at[z], c_z.at[z], cz_s.at[q], cz_r.at[q], along_z(q)))
    pending.append(send(pp.at[e], p_in.at[me], p_s.at[0], p_r.at[me], (e, 8 * c + z)))
    for q in range(1, 16):
        go(remote(pp.at[(e + q) % 16], p_in.at[me], p_s.at[q], p_r.at[me], ((e + q) % 16, 8 * c + z)))
    for q in range(1, 8):
        arrived(c_z.at[(z + 8 - q) % 8], cz_r.at[q])

    def corner_part(q, core):
        return c_all.at[core, :, q // 4, :, pl.ds(pl.multiple_of(128 * (q % 4), 128), 128)]

    for q in range(1, 16):
        go(remote(c_z, corner_part(me, c), cp_s.at[q], cp_r.at[q], in_plane(q)))
    go(remote(c_z, corner_part(me, c), cx_s.at[0], cx_r.at[0], sibling))
    keep = pltpu.make_async_copy(c_z, corner_part(me, c), keep_s)
    keep.start()

    for q in range(1, 16):
        part = corner_part(index_from(q), c)
        arrived(part, cp_r.at[q])
        go(remote(part, part, cx_s.at[q], cx_r.at[q], sibling))
    for q in range(16):
        arrived(p_in.at[q], p_r.at[q])
    total = p_in[0]
    for q in range(1, 16):
        total = total + p_in[q]
    t_own[...] = total
    pending.append(send(t_own, p_rows.at[e], row_s.at[0], row_r.at[e], (p, p)))
    pending.append(send(t_own, p_cols.at[e], col_s.at[0], col_r.at[e], (e, p)))
    for q in range(1, 16):
        go(remote(t_own, p_rows.at[e], row_s.at[q], row_r.at[e], (p, (p + q) % 16)))
        go(remote(t_own, p_cols.at[e], col_s.at[q], col_r.at[e], ((e + q) % 16, p)))
    stay_tt = pltpu.make_async_copy(tt.at[:, pl.ds(pl.multiple_of(16 * me, 16), 16)], tt_in.at[me], tt_r.at[me])
    stay_tt.start()
    for q in range(1, 16):
        rows = pl.ds(pl.multiple_of(16 * index_at(q), 16), 16)
        go(remote(tt.at[:, rows], tt_in.at[me], tt_s.at[q], tt_r.at[me], in_plane(q)))
    keep.wait()
    for q in range(16):
        arrived(corner_part(index_from(q), 1 - c), cx_r.at[q])

    n = a.shape[0]
    a[...] = c_all[...].reshape(n, n)
    ui[:, 128:256] = a[:, pl.ds(pl.multiple_of(128 * (e // 4), 128), 128)]
    def apply(k):
        lo, hi = k * NB, (k + 1) * NB
        inv = inv_ref[k]
        ui[lo:hi, :] = dot_hi(inv, ui[lo:hi, :], ((1,), (0,)))
        uj[lo:hi, :] = dot_hi(inv, uj[lo:hi, :], ((1,), (0,)))
        if hi < n:
            u = a[lo:hi, hi:]
            ui[hi:, :] -= dot_hi(u, ui[lo:hi, :], ((0,), (0,)))
            uj[hi:, :] -= dot_hi(u, uj[lo:hi, :], ((0,), (0,)))

    for k in range(n // NB):
        lo, hi = k * NB, (k + 1) * NB
        d[...] = a[lo:hi, lo:hi]
        inverse_factor(d, inv_ref.at[k])
        if k >= 2:
            apply(k - 1)
        if hi < n:
            a[lo:hi, hi:] = dot_hi(inv_ref[k], a[lo:hi, hi:], ((1,), (0,)))
            u = a[lo:hi, hi:]
            a[hi:, hi:] -= dot_hi(u, u, ((0,), (0,)))
        if k == 1:
            for q in range(16):
                arrived(tt_in.at[q], tt_r.at[q])
            total = tt_in[0]
            for q in range(1, 16):
                total = total + tt_in[q]
            tt_own[...] = total
            part = me % 8
            rows = pl.ds(pl.multiple_of(16 * part, 16), 16)
            for m, kk, to, also in owners:
                pending.append(send(tt_own.at[kk], block.at[rows], blk_s.at[m], blk_r.at[part], to, also))
            for q in range(16):
                arrived(p_rows.at[q], row_r.at[q])
                arrived(p_cols.at[q], col_r.at[q])
            ui[:, 0:128] = p_rows[...].reshape(n, 128)
            uj[...] = p_cols[...].reshape(n, 128)
            apply(0)
    apply(n // NB - 1)
    for t in range(8):
        arrived(block.at[16 * t : 16 * t + 16], blk_r.at[t])
    gram = block[...]
    gram = jnp.where(straight, gram, jnp.transpose(gram))
    same = lax.broadcasted_iota(jnp.int32, (128, 128), 0) == lax.broadcasted_iota(jnp.int32, (128, 128), 1)
    gram = gram + jnp.where(same & (e == p), 1.0, 0.0)
    trail_ref[...] = gram - dot_hi(ui[:, 0:128], uj[...], ((0,), (0,)))
    own_rows = ui[pl.ds(pl.multiple_of(32 * p, 32), 32), :]
    lead = pltpu.roll(own_rows[:, 128:256], (128 - 32 * (e % 4)) % 128, 1)
    rest = pltpu.roll(own_rows[:, 0:128], 32, 1)
    lanes = lax.broadcasted_iota(jnp.int32, (32, 128), 1)
    panel_ref[:, 0:128] = jnp.where(lanes < 32, lead, rest)
    panel_ref[:, 128:160] = rest[:, 0:32]
    for copy in plain:
        copy.wait_send()
    for finish in pending:
        finish()
    drain()
    drain_values()


def fit(desc, points_t, weight):
    dma = pltpu.SemaphoreType.DMA
    vmem = pl.BlockSpec(memory_space=pltpu.VMEM)
    f32 = lambda *shape: pltpu.VMEM(shape, F32)
    bf16 = lambda *shape: pltpu.VMEM(shape, BF16)
    return pl.pallas_call(
        whole,
        out_shape=(jax.ShapeDtypeStruct((32, 160), F32), jax.ShapeDtypeStruct((128, 128), F32)),
        in_specs=[vmem] * 3,
        out_specs=[vmem] * 2,
        scratch_shapes=[
            f32(160, 64), f32(80, 64), f32(1, 1024), f32(384, 128), f32(2, 384, 1024), f32(2, 64, 1024), f32(16, 64, 1024),
            bf16(1024, 1024), bf16(1024, 1024), bf16(768, 1024), bf16(768, 1024),
            f32(2, 8, 2, 16, 1024), f32(3, 2, 2, 64, 1024), f32(5, 256, 128), f32(16, 32, 128), f32(4, 32, 128),
            f32(16, 8, 128), f32(8, 8, 128), f32(2, 8, 4, 8, 512), f32(16, 32, 128), f32(16, 32, 128), f32(16, 32, 128),
            f32(32, 128), f32(16, 5, 16, 128), f32(5, 16, 128), f32(128, 128),
            f32(512, 512), f32(512, 256), f32(512, 128), f32(NB, NB), f32(4, NB, NB),
            dma((3,)), dma((3,)), dma((2,)), dma((2,)),
            dma((8,)), dma((8,)), dma((4,)), dma((4,)),
            dma((16,)), dma((16,)), dma((16,)), dma((16,)),
            dma((16,)), dma((16,)), dma((16,)), dma((16,)),
            dma((4,)), dma((4,)), dma((4,)), dma((4,)),
        ]
        + [dma((16,))] * 8
        + [dma]
        + [dma((16,))] * 10,
        compiler_params=pltpu.CompilerParams(collective_id=0, has_side_effects=True, vmem_limit_bytes=60 * 2**20),
    )(desc, points_t, weight)


def local(descriptors, env_weight, points):
    panel_t, trailing = fit(descriptors, points.T, env_weight.reshape(1, -1))
    return panel_t.T, trailing


def solution(mesh):
    return jax.shard_map(
        local,
        mesh=mesh,
        in_specs=(P("pts", "env"), P("env"), P("pts", "env")),
        out_specs=(P("env", "pts"), P("env", "pts")),
        check_vma=False,
    )
```
